128 devices in a mesh: fsdp: 2 (over y_hi), tile: 32 (over z, x, core), scan: 2 (over y_lo).
Axes of the slice: x: 4, y: 4 (y_hi: 2, y_lo: 2; y = y_hi * 2 + y_lo), z: 4, core: 2. Of those that a mesh axis runs over, the one named last changes fastest.
Arguments:
- acts: bfloat16 [2, 2, 16, 64, 64, 512], P('scan', 'fsdp', None, 'tile'), may hold values from -6 to 6
- spatial_weight: bfloat16 [9, 512, 512], P(None, None, 'fsdp'), may hold values from -0.09375 to 0.09375
- temporal_weight: bfloat16 [3, 512, 512], P(None, None, 'fsdp'), may hold values from -0.15625 to 0.15625
- readout_weight: bfloat16 [2, 4096, 512], P('scan', 'tile'), may hold values from -0.25 to 0.25
- readout_bias: bfloat16 [2, 4096], P('scan', 'tile'), may hold values from -1.5 to 0.5
- tile_of: int32 [2, 4096, 1], P('scan', 'tile'), may hold values from 0 to 31; in each aligned block of 128 rows (0 to 127, 128 to 255, ..., all dimensions but the last counted through in order) at most 10 rows name the same one
- row_of: int32 [2, 4096], P('scan', 'tile'), may hold values from 0 to 1
- column_of: int32 [2, 4096], P('scan', 'tile'), may hold values from 0 to 63
- spikes: int32 [2, 2, 16, 4096], P('scan', 'fsdp', None, 'tile'), may hold values from 0 to 5
Outputs:
- spatial_grad: float32 [9, 512, 512], P(None, None, 'fsdp')
- temporal_grad: float32 [3, 512, 512], P(None, None, 'fsdp')
- readout_grad: float32 [2, 4096, 512], P('scan', 'tile')
- bias_grad: float32 [2, 4096], P('scan', 'tile')
The draws below stay inside these ranges and needn't reach their ends.
Inputs may be any that keep to these rules, and one draw needn't show every extreme that they name: `tile_of`: among the 128 neurons of one index of tile (aligned blocks of a scan's neurons), at most 10 read one tile.
All inputs are finite; a program needn't handle non-finite values.
Results may differ from the reference program's by a relative error of at most 0.006.
Values may be sent and summed in bfloat16 or wider, within the bound.
No kernel may reach another device: no remote copies, remote signals or barrier semaphores. Data moves between devices by JAX's collectives and lax.ppermute only.
A program may use at most 192 MiB of HBM per device.

```python
import math
import jax
import jax.numpy as jnp
import numpy as np
from jax import lax

C = 512
W = 64
FRAMES = 16
ROWS_DEV = 2
NEU_DEV = 128
SCANS = 2
REPS = 2
H = 64
NEU = 4096
CAP = 10
N_TILE = 32


def set_ends(result, own_key, smallest, top_value):
    index_at = [jax.random.randint(jax.random.fold_in(own_key, axis), (), 0, length) for axis, length in enumerate(result.shape)]
    widest = result.shape.index(max(result.shape))
    beside = index_at[:widest] + [(index_at[widest] + 1) % result.shape[widest]] + index_at[widest + 1:]
    return result.at[tuple(index_at)].set(smallest).at[tuple(beside)].set(top_value)


def steps_of(own_key, shape, cuts, least, top_value):
    def one(position, blocks):
        heights = jax.random.uniform(jax.random.fold_in(jax.random.fold_in(own_key, 6), position), (blocks,), jnp.float32, least / len(cuts), top_value / len(cuts))
        return jnp.repeat(jnp.exp(heights), shape[position] // blocks).reshape((-1,) + (1,) * (len(shape) - position - 1))

    factor_of = one(*cuts[0])
    for cut in cuts[1:]:
        factor_of = factor_of * one(*cut)
    return factor_of


def shared_out(rng, own, number, rows, number_of, top, limit, lean):
    sequence = jax.random.permutation(rng, number_of)
    crowded, ordinary = portions_of(number_of, rows * top, limit, lean, True), portions_of(number_of, rows * top, limit, lean, False)
    places = jnp.arange(number_of)

    def named(lengths, offset_by):
        used = int((lengths > 0).sum())
        fixed = max(1, used // 4)
        moved = fixed + (places - fixed + offset_by * (used - fixed)) % max(1, number_of - fixed)
        return jnp.zeros((number_of,), jnp.int32).at[sequence[jnp.where(places < fixed, places, moved)]].set(jnp.asarray(lengths, jnp.int32))

    lengths = jnp.where(number % 4 == 0, named(crowded, number // 4), named(ordinary, number - number // 4 - 1))
    mixed = jax.random.permutation(jax.random.fold_in(own, 3), number_of)
    giver, sink = mixed[0:number_of // 2 * 2:2], mixed[1:number_of // 2 * 2:2]
    room = jnp.minimum(lengths[giver] - 1, limit - lengths[sink]) // 2
    room = jnp.where((giver == sequence[0]) | (sink == sequence[0]) | (lengths[sink] == 0), 0, jnp.maximum(room, 0))
    moved = jax.random.randint(jax.random.fold_in(own, 4), (number_of // 2,), 0, 1 << 20) % (room + 1)
    lengths = lengths.at[giver].add(-moved).at[sink].add(moved)
    items = jnp.searchsorted(jnp.cumsum(lengths), jnp.arange(rows * top), side="right").astype(jnp.int32)
    table = items.reshape(top, rows).T
    table = table[jax.random.permutation(jax.random.fold_in(own, 1), rows)]
    offset_by = jax.random.randint(jax.random.fold_in(own, 2), (rows, 1), 0, top)
    return jnp.take_along_axis(table, (jnp.arange(top)[None, :] + offset_by) % top, axis=1)


def portions_of(number_of, total, bound, skew, full):
    portions = [(1 << 20) // math.isqrt(standing ** skew) + 1 for standing in range(1, number_of + 1)]
    largest = bound if full else min(bound, max(-(-total // number_of), total * portions[0] // sum(portions)))
    least = 1 if total - largest >= number_of - 1 else 0
    holding, rest = [largest] + [least] * (number_of - 1), total - largest - least * (number_of - 1)
    while rest > 0:
        candidates = [i for i in range(1, number_of) if holding[i] < largest] or [i for i in range(1, number_of) if holding[i] < bound]
        mass, remaining = sum([portions[i] for i in candidates]), rest
        for i in candidates:
            extra = min(bound - holding[i], max(1, remaining * portions[i] // mass), rest)
            holding[i] = holding[i] + extra
            rest = rest - extra
    return np.array(holding)


def normal_values(key, dims, deviation, limit, split=(), kind=jnp.bfloat16):
    factor_of = steps_of(key, dims, split, -0.22, 0.18) if split else 1.0
    drawn = jax.random.normal(key, dims, jnp.float32) * deviation * factor_of
    return jnp.minimum(jnp.maximum(drawn, -limit), limit).astype(kind)


def setup_inputs(seed: int = 0) -> dict:
    keys = jax.random.split(jax.random.key(seed), 10)
    acts = normal_values(keys[0], (SCANS, REPS, FRAMES, H, W, C), 1.0, 6.0, ((0, 2), (1, 2), (3, 32)))
    spatial_weight = normal_values(keys[1], (9, C, C), (9 * C) ** -0.5, 0.09375, ((2, 2),))
    temporal_weight = normal_values(keys[2], (3, C, C), (3 * C) ** -0.5, 0.15625, ((2, 2),))
    readout_weight = normal_values(keys[3], (SCANS, NEU, C), C ** -0.5, 0.25, ((0, 2), (1, 32)))
    readout_bias = jnp.clip(-1.5 + 2.0 * jax.random.uniform(keys[4], (SCANS, NEU), jnp.float32) ** steps_of(keys[4], (SCANS, NEU), ((0, 2), (1, 32)), -0.2, 0.2), -1.5, 0.5).astype(jnp.bfloat16)
    tile_of_keys = jax.random.split(jax.random.fold_in(keys[5], 1), SCANS * NEU // NEU_DEV)
    tile_of_turns = jax.random.permutation(jax.random.fold_in(keys[5], 3), SCANS * NEU // NEU_DEV)
    tile_of = jax.vmap(lambda own, number: shared_out(jax.random.fold_in(keys[5], 2), own, number, NEU_DEV, N_TILE, 1, CAP, 2))(tile_of_keys, tile_of_turns).reshape((SCANS, NEU, 1))
    row_of = set_ends(jax.random.randint(keys[6], (SCANS, NEU), 0, ROWS_DEV), jax.random.fold_in(keys[6], 1), 0, ROWS_DEV - 1).astype(jnp.int32)
    column_of = set_ends(jax.random.randint(keys[7], (SCANS, NEU), 0, W), jax.random.fold_in(keys[7], 1), 0, W - 1).astype(jnp.int32)
    spikes = set_ends(jax.random.randint(keys[8], (SCANS, REPS, FRAMES, NEU), 0, 6), jax.random.fold_in(keys[8], 1), 0, 5).astype(jnp.int32)
    return dict(acts=acts, spatial_weight=spatial_weight, temporal_weight=temporal_weight, readout_weight=readout_weight, readout_bias=readout_bias, tile_of=tile_of, row_of=row_of, column_of=column_of, spikes=spikes)


def hold_bf16(values):
    return lax.optimization_barrier(values.astype(jnp.bfloat16)).astype(jnp.float32)


def reference(acts, spatial_weight, temporal_weight, readout_weight, readout_bias, tile_of, row_of, column_of, spikes):
    spatial = spatial_weight.astype(jnp.float32)
    temporal = temporal_weight.astype(jnp.float32)
    spatial_grad = jnp.zeros((9, C, C), jnp.float32)
    temporal_grad = jnp.zeros((3, C, C), jnp.float32)
    readout_list = []
    bias_list = []
    scale_factor = 1.0 / (REPS * FRAMES)
    for scan_index in range(SCANS):
        rows_global = (tile_of[scan_index, :, 0] * ROWS_DEV + row_of[scan_index]).astype(jnp.int32)
        columns = column_of[scan_index].astype(jnp.int32)
        weights_now = readout_weight[scan_index].astype(jnp.float32)
        bias_now = readout_bias[scan_index].astype(jnp.float32)
        weight_acc = jnp.zeros((NEU, C), jnp.float32)
        bias_acc = jnp.zeros((NEU,), jnp.float32)
        for clip_index in range(REPS):
            frames_in = acts[scan_index, clip_index].astype(jnp.float32)
            padded = jnp.pad(frames_in, ((0, 0), (1, 1), (1, 1), (0, 0)))
            spatial_out = jnp.zeros((FRAMES, H, W, C), jnp.float32)
            for tap in range(9):
                row_tap = tap // 3
                col_tap = tap % 3
                spatial_out = spatial_out + jnp.einsum('fhwc,cd->fhwd', padded[:, row_tap:row_tap + H, col_tap:col_tap + W, :], spatial[tap])
            spatial_out = hold_bf16(spatial_out)
            causal = jnp.pad(spatial_out, ((2, 0), (0, 0), (0, 0), (0, 0)))
            mixed = jnp.zeros((FRAMES, H, W, C), jnp.float32)
            for lag in range(3):
                mixed = mixed + jnp.einsum('fhwc,cd->fhwd', causal[2 - lag:2 - lag + FRAMES], temporal[lag])
            features = hold_bf16(jax.nn.elu(mixed))
            picked = features[:, rows_global, columns, :]
            logits = jnp.einsum('fnc,nc->fn', picked, weights_now) + bias_now[None, :]
            delta = (jnp.exp(logits) - spikes[scan_index, clip_index].astype(jnp.float32)) * scale_factor
            weight_acc = weight_acc + jnp.einsum('fn,fnc->nc', delta, picked)
            bias_acc = bias_acc + jnp.sum(delta, axis=0)
            terms = hold_bf16(delta[:, :, None] * weights_now[None, :, :])
            feature_grad = jnp.zeros((FRAMES, H, W, C), jnp.float32).at[:, rows_global, columns, :].add(terms)
            slope = jnp.where(mixed > 0, 1.0, jnp.exp(jnp.minimum(mixed, 0.0)))
            mixed_grad = hold_bf16(feature_grad * slope)
            for lag in range(3):
                temporal_grad = temporal_grad.at[lag].add(jnp.einsum('fhwc,fhwd->cd', causal[2 - lag:2 - lag + FRAMES], mixed_grad))
            back_pad = jnp.pad(mixed_grad, ((0, 2), (0, 0), (0, 0), (0, 0)))
            spatial_back = jnp.zeros((FRAMES, H, W, C), jnp.float32)
            for lag in range(3):
                spatial_back = spatial_back + jnp.einsum('fhwd,cd->fhwc', back_pad[lag:lag + FRAMES], temporal[lag])
            spatial_back = hold_bf16(spatial_back)
            for tap in range(9):
                row_tap = tap // 3
                col_tap = tap % 3
                spatial_grad = spatial_grad.at[tap].add(jnp.einsum('fhwc,fhwd->cd', padded[:, row_tap:row_tap + H, col_tap:col_tap + W, :], spatial_back))
        readout_list.append(weight_acc)
        bias_list.append(bias_acc)
    return spatial_grad, temporal_grad, jnp.stack(readout_list), jnp.stack(bias_list)
```

```python
import jax
import jax.numpy as jnp
from jax import lax
from jax.sharding import Mesh, PartitionSpec as P

BF = jnp.bfloat16
F32 = jnp.float32
TILE = ("z", "x", "core")
PACK = 640


def contract_rows(left, right):
    return lax.dot_general(left, right, (((0,), (0,)), ((), ())), preferred_element_type=F32)


def swap(value, axis, kind):
    if axis == "core":
        pairs = ((0, 1),)
    elif kind == 0:
        pairs = ((0, 1), (2, 3))
    else:
        pairs = ((1, 2), (3, 0))
    name = ("fsdp", "scan") if axis == "y" else axis
    perm = [pair for a, b in pairs for pair in ((a, b), (b, a))]
    return lax.ppermute(value, name, perm)


def bit(axis, kind):
    if axis == "core":
        return lax.axis_index("core")
    if axis == "y":
        place = lax.axis_index("fsdp") * 2 + lax.axis_index("scan")
    else:
        place = lax.axis_index(axis)
    return place >> 1 if kind else (place ^ (place >> 1)) & 1


def halve(value, axis, kind, dim=0):
    size = value.shape[dim] // 2
    mine = bit(axis, kind)
    sent = lax.dynamic_slice_in_dim(value, (1 - mine) * size, size, dim)
    kept = lax.dynamic_slice_in_dim(value, mine * size, size, dim)
    return kept.astype(F32) + swap(sent.astype(BF), axis, kind).astype(F32)


def double(value, axis, kind, dim=0):
    other = swap(value, axis, kind)
    first = bit(axis, kind) == 0
    return jnp.concatenate(
        [jnp.where(first, value, other), jnp.where(first, other, value)], axis=dim
    )


ORDERS = (("x", "y", "z"), ("y", "z", "x"), ("x", "y", "z"), ("y", "z", "x"))


def reduce_slice(grad, order):
    value = halve(grad, "core", 0)
    for axis in order:
        value = halve(value, axis, 0)
    return value


def finish(slices):
    value = halve(jnp.stack(slices), "y", 1, 2)
    value = halve(halve(value, "x", 1), "z", 1).astype(BF)
    value = double(double(value, "z", 1), "x", 1)
    pairs = []
    for first in range(2):
        pair = jnp.stack([value[first], value[first + 2]])
        for axis in reversed(ORDERS[first]):
            pair = double(pair, axis, 0, 1)
        pairs.append(pair)
    return double(jnp.stack(pairs, axis=1), "core", 0, 2).astype(F32)


def other_half(spatial, temporal):
    color = bit("x", 0) ^ (bit("x", 1) * 2) ^ (bit("z", 0) * 3)
    rows = spatial.shape[1] // 2
    start = lax.axis_index("core") * rows
    taps = lax.dynamic_slice(
        spatial, (3 * jnp.minimum(color, 2), start, 0), (3, rows, spatial.shape[2])
    )
    lags = lax.dynamic_slice_in_dim(temporal, start, rows, 1)
    part = swap(jnp.where(color == 3, lags, taps), "y", 1)
    parts = jnp.stack([part, swap(part, "x", 0), swap(part, "x", 1), swap(part, "z", 0)])
    parts = jnp.stack([lax.dynamic_index_in_dim(parts, p ^ color, 0, False) for p in range(4)])
    whole = double(parts, "core", 0, 2)
    return whole[:3].reshape(spatial.shape), whole[3]


def halo(block):
    count = 1
    for axis in TILE:
        count *= lax.axis_size(axis)
    forward = [(i, i + 1) for i in range(count - 1)]
    backward = [(b, a) for a, b in forward]
    low = lax.ppermute(block[:, -1:], TILE, forward)
    high = lax.ppermute(block[:, :1], TILE, backward)
    return jnp.concatenate([low, block, high], axis=1)


def on_device(
    acts,
    spatial_weight,
    temporal_weight,
    readout_weight,
    readout_bias,
    tile_of,
    row_of,
    column_of,
    spikes,
):
    first = lax.axis_index("fsdp") == 0
    spatial, temporal = (
        jnp.concatenate([jnp.where(first, own, far), jnp.where(first, far, own)], axis=2)
        for own, far in zip(
            (spatial_weight, temporal_weight), other_half(spatial_weight, temporal_weight)
        )
    )
    frames_in = acts[0, 0]
    frames, rows, width, channels = frames_in.shape
    cells = rows * width
    tile_count = lax.axis_size("z") * lax.axis_size("x") * lax.axis_size("core")
    rep_count = lax.axis_size("fsdp")
    neurons = readout_weight.shape[1]
    capacity = max(2, 5 * neurons // (2 * tile_count))
    slot_count = tile_count * capacity
    scale_factor = 1.0 / (rep_count * frames)

    tile_ids = tile_of[0, :, 0]
    cell_ids = row_of[0] * width + column_of[0]
    same_tile = tile_ids[:, None] == tile_ids[None, :]
    order = jnp.arange(neurons)
    rank_ids = jnp.sum((same_tile & (order[None, :] < order[:, None])).astype(jnp.int32), axis=1)
    slot_ids = tile_ids * capacity + rank_ids
    selector = (slot_ids[None, :] == jnp.arange(slot_count)[:, None]).astype(BF)
    table = jnp.concatenate(
        [
            readout_weight[0],
            readout_bias[0][:, None],
            cell_ids.astype(BF)[:, None],
            jnp.ones((neurons, 1), BF),
            spikes[0, 0].T.astype(BF),
            jnp.zeros((neurons, PACK - channels - 3 - frames), BF),
        ],
        axis=1,
    )
    packed = jnp.dot(selector, table, preferred_element_type=F32).astype(BF)
    held = lax.all_to_all(
        packed.reshape(tile_count, capacity, PACK), TILE, split_axis=0, concat_axis=0, tiled=True
    ).reshape(slot_count, PACK)
    slot_weight = held[:, :channels]
    extras = held[:, channels : channels + 3 + frames].astype(F32)
    slot_bias = extras[:, 0]
    slot_cell = jnp.where(extras[:, 2] > 0.5, extras[:, 1].astype(jnp.int32), cells)
    slot_spikes = extras[:, 3:].T

    extended = halo(frames_in)
    padded = jnp.pad(extended, ((0, 0), (0, 0), (1, 1), (0, 0)))

    def patch(tap):
        return padded[:, tap // 3 : tap // 3 + rows, tap % 3 : tap % 3 + width, :].reshape(
            -1, channels
        )

    spatial_sum = jnp.zeros((frames * cells, channels), F32)
    for tap in range(9):
        spatial_sum = spatial_sum + jnp.dot(patch(tap), spatial[tap], preferred_element_type=F32)
    spatial_out = spatial_sum.astype(BF).reshape(frames, cells, channels)
    causal = jnp.pad(spatial_out, ((2, 0), (0, 0), (0, 0)))
    mixed = jnp.zeros((frames * cells, channels), F32)
    for lag in range(3):
        mixed = mixed + jnp.dot(
            causal[2 - lag : 2 - lag + frames].reshape(-1, channels),
            temporal[lag],
            preferred_element_type=F32,
        )
    features = jax.nn.elu(mixed).astype(BF)

    here = jnp.arange(cells)[:, None] == slot_cell[None, :]
    scores = lax.dot_general(
        features, slot_weight, (((1,), (1,)), ((), ())), preferred_element_type=F32
    ).reshape(frames, cells, slot_count)
    logits = jnp.sum(jnp.where(here[None], scores, 0.0), axis=1) + slot_bias[None, :]
    delta = (jnp.exp(logits) - slot_spikes) * scale_factor
    spread = jnp.where(here[None], delta[:, None, :], 0.0).astype(BF).reshape(-1, slot_count)
    slot_grad = contract_rows(spread, features)
    slot_bias_grad = jnp.sum(delta, axis=0)
    back = jnp.concatenate(
        [slot_grad, slot_bias_grad[:, None], jnp.zeros((slot_count, PACK - channels - 1), F32)],
        axis=1,
    ).astype(BF)
    returned = lax.all_to_all(
        back.reshape(tile_count, capacity, PACK), TILE, split_axis=0, concat_axis=0, tiled=True
    ).reshape(slot_count, PACK)
    mine = contract_rows(selector, returned)
    other = lax.ppermute(mine.astype(BF), "fsdp", [(0, 1), (1, 0)])
    summed = mine + other.astype(F32)
    weight_grad = summed[:, :channels]
    bias_grad = summed[:, channels]

    feature_grad = jnp.dot(spread, slot_weight, preferred_element_type=F32)
    slope = jnp.where(mixed > 0, 1.0, jnp.exp(jnp.minimum(mixed, 0.0)))
    mixed_grad = (feature_grad * slope).astype(BF)
    slices = [
        reduce_slice(
            jnp.concatenate(
                [
                    contract_rows(causal[2 - lag : 2 - lag + frames].reshape(-1, channels), mixed_grad)
                    for lag in range(3)
                ]
            ),
            ORDERS[0],
        )
    ]
    back_pad = jnp.pad(mixed_grad.reshape(frames, cells, channels), ((0, 2), (0, 0), (0, 0)))
    spatial_back = jnp.zeros((frames * cells, channels), F32)
    for lag in range(3):
        spatial_back = spatial_back + lax.dot_general(
            back_pad[lag : lag + frames].reshape(-1, channels),
            temporal[lag],
            (((1,), (1,)), ((), ())),
            preferred_element_type=F32,
        )
    spatial_back = spatial_back.astype(BF)
    for group in range(3):
        grads = [contract_rows(patch(3 * group + tap), spatial_back) for tap in range(3)]
        slices.append(reduce_slice(jnp.concatenate(grads), ORDERS[group + 1]))
    total = finish(slices)
    shape = (3, channels, channels // 2)
    total_temporal = total[0, 0].reshape(shape)
    total_spatial = jnp.concatenate(
        [total[0, 1].reshape(shape), total[1, 0].reshape(shape), total[1, 1].reshape(shape)]
    )
    return (total_spatial, total_temporal, weight_grad[None], bias_grad[None])


def solution(mesh):
    shape = mesh.devices.shape
    split = Mesh(
        mesh.devices.reshape(shape[0], 4, 4, 2, shape[2]), ("fsdp", "z", "x", "core", "scan")
    )
    return jax.shard_map(
        on_device,
        mesh=split,
        in_specs=(
            P("scan", "fsdp", None, TILE, None, None),
            P(None, None, "fsdp"),
            P(None, None, "fsdp"),
            P("scan", TILE, None),
            P("scan", TILE),
            P("scan", TILE, None),
            P("scan", TILE),
            P("scan", TILE),
            P("scan", "fsdp", None, TILE),
        ),
        out_specs=(
            P(None, None, "fsdp"),
            P(None, None, "fsdp"),
            P("scan", TILE, None),
            P("scan", TILE),
        ),
        check_vma=False,
    )
```

```python
import jax
import jax.numpy as jnp
from jax import lax
from jax.sharding import Mesh, PartitionSpec as P


BF = jnp.bfloat16
F32 = jnp.float32
TILE = ("z", "x", "core")
PACK = 640


def contract_rows(left, right):
    return lax.dot_general(left, right, (((0,), (0,)), ((), ())), preferred_element_type=F32)


def swap(value, axis, kind):
    if axis == "core":
        pairs = ((0, 1),)
    elif kind == 0:
        pairs = ((0, 1), (2, 3))
    else:
        pairs = ((1, 2), (3, 0))
    name = ("fsdp", "scan") if axis == "y" else axis
    perm = [pair for a, b in pairs for pair in ((a, b), (b, a))]
    return lax.ppermute(value, name, perm)


def bit(axis, kind):
    if axis == "core":
        return lax.axis_index("core")
    if axis == "y":
        place = lax.axis_index("fsdp") * 2 + lax.axis_index("scan")
    else:
        place = lax.axis_index(axis)
    return place >> 1 if kind else (place ^ (place >> 1)) & 1


def halve(value, axis, kind, flip=0):
    size = value.shape[0] // 2
    mine = bit(axis, kind) ^ flip
    sent = lax.dynamic_slice_in_dim(value, (1 - mine) * size, size, 0)
    kept = lax.dynamic_slice_in_dim(value, mine * size, size, 0)
    return kept.astype(F32) + swap(sent.astype(BF), axis, kind).astype(F32)


def own_columns(value):
    cols = value.shape[1] // 6
    own, far = (
        jnp.concatenate([value[:, (2 * g + h) * cols :][:, :cols] for g in range(3)], axis=1)
        for h in range(2)
    )
    return own.astype(F32) + swap(far.astype(BF), "y", 1).astype(F32)


def share(value, axis, kind):
    value = value.astype(BF)
    return value.astype(F32) + swap(value, axis, kind).astype(F32)


def double(value, axis, kind, dim):
    other = swap(value, axis, kind)
    first = bit(axis, kind) == 0
    return jnp.concatenate(
        [jnp.where(first, value, other), jnp.where(first, other, value)], axis=dim
    )


def blocks_of(spatial, temporal):
    color = bit("x", 0) ^ (bit("x", 1) * 2) ^ (bit("z", 0) * 3)
    rows, cols = spatial.shape[1] // 2, spatial.shape[2]
    core = lax.axis_index("core")
    start = core * rows
    taps = lax.dynamic_slice(spatial, (3 * jnp.minimum(color, 2), start, 0), (3, rows, cols))
    lags = lax.dynamic_slice_in_dim(temporal, start, rows, 1)
    part = jnp.where(color == 3, lags, taps)
    part = jnp.concatenate([part[0], part[1], part[2]], axis=1)
    part = swap(part, "y", 1)
    parts = [part, swap(part, "x", 0), swap(part, "x", 1), swap(part, "z", 0)]
    mine = jnp.stack(parts)
    other = swap(mine, "core", 0)
    both = jnp.stack([mine, other])

    def block(half, group):
        index = (half ^ core, group ^ color, 0, 0)
        return lax.dynamic_slice(both, index, (1, 1, rows, 3 * cols))[0, 0]

    return block


def edges(block):
    count = 1
    for axis in TILE:
        count *= lax.axis_size(axis)
    forward = [(i, i + 1) for i in range(count - 1)]
    backward = [(b, a) for a, b in forward]
    low = lax.ppermute(block[:, -1:], TILE, forward)
    high = lax.ppermute(block[:, :1], TILE, backward)
    return low, high


def shift(value, step):
    if step == 0:
        return value
    zeros = jnp.zeros_like(value[:, :, :1])
    if step > 0:
        return jnp.concatenate([value[:, :, 1:], zeros], axis=2)
    return jnp.concatenate([zeros, value[:, :, :-1]], axis=2)


def compute(
    acts,
    spatial_weight,
    temporal_weight,
    readout_weight,
    readout_bias,
    tile_of,
    row_of,
    column_of,
    spikes,
):
    fsdp = lax.axis_index("fsdp")
    block = blocks_of(spatial_weight, temporal_weight)
    frames_in = acts[0, 0]
    frames, rows, width, channels = frames_in.shape
    half = channels // 2
    cells = rows * width
    tile_count = lax.axis_size("z") * lax.axis_size("x") * lax.axis_size("core")
    rep_count = lax.axis_size("fsdp")
    neurons = readout_weight.shape[1]
    capacity = max(2, 5 * neurons // (2 * tile_count))
    slot_count = tile_count * capacity
    scale_factor = 1.0 / (rep_count * frames)
    low, high = edges(frames_in)

    def local(value):
        return jnp.where(
            fsdp == 0, value, jnp.concatenate([value[:, half:], value[:, :half]], axis=1)
        )

    tile_ids = tile_of[0, :, 0]
    cell_ids = row_of[0] * width + column_of[0]
    same_tile = tile_ids[:, None] == tile_ids[None, :]
    order = jnp.arange(neurons)
    rank_ids = jnp.sum((same_tile & (order[None, :] < order[:, None])).astype(jnp.int32), axis=1)
    slot_ids = tile_ids * capacity + rank_ids
    selector = (slot_ids[None, :] == jnp.arange(slot_count)[:, None]).astype(BF)
    table = jnp.concatenate(
        [
            local(readout_weight[0]),
            readout_bias[0][:, None],
            cell_ids.astype(BF)[:, None],
            jnp.ones((neurons, 1), BF),
            spikes[0, 0].T.astype(BF),
            jnp.zeros((neurons, PACK - channels - 3 - frames), BF),
        ],
        axis=1,
    )
    packed = jnp.dot(selector, table, preferred_element_type=F32).astype(BF)
    held = lax.all_to_all(
        packed.reshape(tile_count, capacity, PACK),
        TILE,
        split_axis=0,
        concat_axis=0,
        tiled=True,
    ).reshape(slot_count, PACK)
    slot_weight = held[:, :channels]
    extras = held[:, channels : channels + 3 + frames].astype(F32)
    slot_bias = extras[:, 0]
    slot_cell = jnp.where(extras[:, 2] > 0.5, extras[:, 1].astype(jnp.int32), cells)
    slot_spikes = extras[:, 3:].T

    shifted_rows = [
        jnp.concatenate([low, frames_in[:, :1]], axis=1).reshape(-1, channels),
        frames_in.reshape(-1, channels),
        jnp.concatenate([frames_in[:, 1:], high], axis=1).reshape(-1, channels),
    ]
    taller = jnp.concatenate(shifted_rows, axis=1)

    def convolve(weights):
        sums = jnp.dot(taller, weights, preferred_element_type=F32)
        sums = sums.reshape(frames, rows, width, 3 * half)
        total = (
            shift(sums[..., :half], -1)
            + sums[..., half : 2 * half]
            + shift(sums[..., 2 * half :], 1)
        )
        return total.astype(BF).reshape(frames, cells, half)

    near_weights = jnp.concatenate(
        [
            jnp.concatenate([spatial_weight[3 * a + b] for b in range(3)], axis=1)
            for a in range(3)
        ]
    )
    near_out = convolve(near_weights)
    far_out = convolve(jnp.concatenate([block(h, g) for g in range(3) for h in range(2)]))
    spatial_out = jnp.concatenate([near_out, far_out], axis=2)

    lag_blocks = [block(q ^ fsdp, 3) for q in range(2)]
    temporal = [
        jnp.concatenate(
            [
                jnp.concatenate(
                    [
                        lax.dynamic_slice_in_dim(temporal_weight[lag], (q ^ fsdp) * half, half, 0),
                        lag_blocks[q][:, lag * half : (lag + 1) * half],
                    ],
                    axis=1,
                )
                for q in range(2)
            ]
        )
        for lag in range(3)
    ]
    causal = jnp.pad(spatial_out, ((2, 0), (0, 0), (0, 0)))
    mixed = jnp.zeros((frames * cells, channels), F32)
    for lag in range(3):
        mixed = mixed + jnp.dot(
            causal[2 - lag : 2 - lag + frames].reshape(-1, channels),
            temporal[lag],
            preferred_element_type=F32,
        )
    features = jax.nn.elu(mixed).astype(BF)

    here = jnp.arange(cells)[:, None] == slot_cell[None, :]
    scores = lax.dot_general(
        features, slot_weight, (((1,), (1,)), ((), ())), preferred_element_type=F32
    ).reshape(frames, cells, slot_count)
    logits = jnp.sum(jnp.where(here[None], scores, 0.0), axis=1) + slot_bias[None, :]
    delta = (jnp.exp(logits) - slot_spikes) * scale_factor
    spread = jnp.where(here[None], delta[:, None, :], 0.0).astype(BF).reshape(-1, slot_count)
    feature_grad = jnp.dot(spread, slot_weight, preferred_element_type=F32)
    slope = jnp.where(mixed > 0, 1.0, jnp.exp(jnp.minimum(mixed, 0.0)))
    mixed_grad = (feature_grad * slope).astype(BF)
    back_pad = jnp.pad(mixed_grad.reshape(frames, cells, channels), ((0, 2), (0, 0), (0, 0)))
    later = jnp.concatenate(
        [back_pad[lag : lag + frames].reshape(-1, channels) for lag in range(3)], axis=1
    )
    grad_t = contract_rows(spatial_out.reshape(-1, channels), later)
    part_t = halve(grad_t, "core", 0, fsdp)

    slot_grad = contract_rows(spread, features)
    slot_bias_grad = jnp.sum(delta, axis=0)
    back = jnp.concatenate(
        [slot_grad, slot_bias_grad[:, None], jnp.zeros((slot_count, PACK - channels - 1), F32)],
        axis=1,
    ).astype(BF)

    spatial_back = lax.dot_general(
        later,
        jnp.concatenate(temporal, axis=1),
        (((1,), (1,)), ((), ())),
        preferred_element_type=F32,
    )
    spatial_back = spatial_back.reshape(frames, rows, width, channels)
    wider = jnp.concatenate(
        [shift(spatial_back, 1 - b).astype(BF).reshape(-1, channels) for b in range(3)], axis=1
    )
    part_t = halve(part_t, "x", 0)
    grad_0 = contract_rows(shifted_rows[0], wider)
    part_0 = halve(grad_0, "core", 0)
    grad_1 = contract_rows(shifted_rows[1], wider)
    part_1 = halve(grad_1, "core", 0)
    part_0 = own_columns(part_0)
    grad_2 = contract_rows(shifted_rows[2], wider)
    part_2 = halve(grad_2, "core", 0)
    part_t = halve(part_t, "y", 0)
    part_1 = halve(part_1, "x", 0)
    part_2 = own_columns(part_2)
    part_t = halve(part_t, "z", 0)
    part_0 = halve(part_0, "x", 1)
    part_1 = halve(part_1, "y", 0)
    part_0 = halve(part_0, "z", 1)
    part_2 = halve(part_2, "x", 1)
    part_1 = halve(part_1, "z", 0)
    part_2 = halve(part_2, "z", 1)

    returned = lax.all_to_all(
        back.reshape(tile_count, capacity, PACK), TILE, split_axis=0, concat_axis=0, tiled=True
    ).reshape(slot_count, PACK)
    mine = contract_rows(selector, returned)
    mine = jnp.concatenate([local(mine[:, :channels]), mine[:, channels:]], axis=1).astype(BF)
    other = lax.ppermute(mine, "fsdp", [(0, 1), (1, 0)])
    summed = mine.astype(F32) + other.astype(F32)
    weight_grad = summed[:, :channels]
    bias_grad = summed[:, channels]

    odd = jnp.concatenate([part_t, part_1])
    even = jnp.concatenate([part_0, part_2])
    odd = own_columns(odd)
    even = share(even, "x", 0)
    odd = share(odd, "x", 1)
    even = share(even, "y", 0)
    odd = share(odd, "z", 1)
    even = share(even, "z", 0)
    odd = odd.astype(BF).reshape(2, -1, odd.shape[1])
    even = even.astype(BF).reshape(2, -1, even.shape[1])
    odd = double(odd, "z", 0, 1)
    even = double(even, "z", 1, 1)
    odd = double(odd, "y", 0, 1)
    even = double(even, "x", 1, 1)
    odd = double(odd, "x", 0, 1)
    even = double(even, "core", 0, 1)
    odd = double(odd, "core", 0, 1)

    def taps(value):
        return [value[:, b * half : (b + 1) * half].astype(F32) for b in range(3)]

    total_temporal = jnp.stack(taps(odd[0]))
    total_spatial = jnp.stack(taps(even[0]) + taps(odd[1]) + taps(even[1]))
    return (total_spatial, total_temporal, weight_grad[None], bias_grad[None])


def solution(mesh):
    shape = mesh.devices.shape
    split = Mesh(
        mesh.devices.reshape(shape[0], 4, 4, 2, shape[2]), ("fsdp", "z", "x", "core", "scan")
    )
    return jax.shard_map(
        compute,
        mesh=split,
        in_specs=(
            P("scan", "fsdp", None, TILE, None, None),
            P(None, None, "fsdp"),
            P(None, None, "fsdp"),
            P("scan", TILE, None),
            P("scan", TILE),
            P("scan", TILE, None),
            P("scan", TILE),
            P("scan", TILE),
            P("scan", "fsdp", None, TILE),
        ),
        out_specs=(
            P(None, None, "fsdp"),
            P(None, None, "fsdp"),
            P("scan", TILE, None),
            P("scan", TILE),
        ),
        check_vma=False,
    )
```

```python
import math

import jax
import jax.numpy as jnp
from jax import lax
from jax.sharding import Mesh, PartitionSpec as P


BF = jnp.bfloat16
F32 = jnp.float32
TILE = ("z", "x", "core")
ALL = ("fsdp", "z", "x", "core", "scan")
PACK = 640


def contract_rows(left, right):
    return lax.dot_general(left, right, (((0,), (0,)), ((), ())), preferred_element_type=F32)


def swap(value, axis, kind):
    if axis == "core":
        pairs = ((0, 1),)
    elif kind == 0:
        pairs = ((0, 1), (2, 3))
    else:
        pairs = ((1, 2), (3, 0))
    name = ("fsdp", "scan") if axis == "y" else axis
    perm = [pair for a, b in pairs for pair in ((a, b), (b, a))]
    return lax.ppermute(value, name, perm)


def bit(axis, kind):
    if axis == "core":
        return lax.axis_index("core")
    if axis == "y":
        place = lax.axis_index("fsdp") * 2 + lax.axis_index("scan")
    else:
        place = lax.axis_index(axis)
    return place >> 1 if kind else (place ^ (place >> 1)) & 1


def partner(dim, place):
    _, kind = dim
    if kind == 0:
        return place ^ 1
    return (place + (1 if place & 1 else -1)) % 4


def swap_by_core(value, dims):
    sizes = [lax.axis_size(name) for name in ALL]
    perm = []
    for index in range(math.prod(sizes)):
        rest, spot = index, {}
        for name, size in zip(reversed(ALL), reversed(sizes)):
            spot[name] = rest % size
            rest //= size
        spot["y"] = spot["fsdp"] * 2 + spot["scan"]
        dim = dims[spot["core"]]
        spot[dim[0]] = partner(dim, spot[dim[0]])
        spot["fsdp"], spot["scan"] = spot["y"] // 2, spot["y"] % 2
        target = 0
        for name, size in zip(ALL, sizes):
            target = target * size + spot[name]
        perm.append((index, target))
    return lax.ppermute(value, ALL, perm)


def bit_by_core(dims):
    return jnp.where(lax.axis_index("core") == 0, bit(*dims[0]), bit(*dims[1]))


def halve(value, dims):
    size = value.shape[1] // 2
    mine = bit_by_core(dims)
    sent = lax.dynamic_slice_in_dim(value, (1 - mine) * size, size, 1)
    kept = lax.dynamic_slice_in_dim(value, mine * size, size, 1)
    return kept + swap_by_core(sent.astype(BF), dims).astype(F32)


def own_columns(value):
    cols = value.shape[2] // 6
    own, far = (
        jnp.concatenate([value[:, :, (2 * g + h) * cols :][:, :, :cols] for g in range(3)], axis=2)
        for h in range(2)
    )
    return own + swap(far.astype(BF), "y", 1).astype(F32)


def joined(value, other, mine):
    first = mine == 0
    return jnp.concatenate(
        [jnp.where(first, value, other), jnp.where(first, other, value)], axis=1
    )


XA, XB, YA, ZA, ZB = ("x", 0), ("x", 1), ("y", 0), ("z", 0), ("z", 1)
STEPS = {
    "s1": ((XA, XB), (XB, XA), (YA, YA), (ZA, ZB), (ZB, ZA)),
    "s2": ((ZA, ZB), (ZB, ZA), (YA, YA), (XA, XB), (XB, XA)),
}


def reduce_first(grads, flips):
    core = lax.axis_index("core")
    size = grads[0].shape[0] // 2
    kept, sent = (
        jnp.stack(
            [
                lax.dynamic_slice_in_dim(grad, (core ^ flip ^ far) * size, size, 0)
                for grad, flip in zip(grads, flips)
            ]
        )
        for far in range(2)
    )
    return kept + swap(sent.astype(BF), "core", 0).astype(F32)


def reduce_rest(name, value):
    steps = STEPS[name]
    for index in range(3):
        value = halve(value, steps[index])
    value = own_columns(value)
    for index in range(3, 5):
        value = value + swap_by_core(value, steps[index])
    value = value.astype(BF)
    for index in (2, 1, 0):
        other = swap_by_core(value, steps[index])
        value = joined(value, other, bit_by_core(steps[index]))
    return joined(value, swap(value, "core", 0), lax.axis_index("core"))


def blocks_of(spatial, temporal):
    color = bit("x", 0) ^ (bit("x", 1) * 2) ^ (bit("z", 0) * 3)
    rows, cols = spatial.shape[1] // 2, spatial.shape[2]
    core = lax.axis_index("core")
    start = core * rows
    taps = lax.dynamic_slice(spatial, (3 * jnp.minimum(color, 2), start, 0), (3, rows, cols))
    lags = lax.dynamic_slice_in_dim(temporal, start, rows, 1)
    part = jnp.where(color == 3, lags, taps)
    part = jnp.concatenate([part[0], part[1], part[2]], axis=1)
    part = swap(part, "y", 1)
    parts = [part, swap(part, "x", 0), swap(part, "x", 1), swap(part, "z", 0)]
    mine = jnp.stack(parts)
    other = swap(mine, "core", 0)
    both = jnp.stack([mine, other])

    def block(half, group):
        index = (half ^ core, group ^ color, 0, 0)
        return lax.dynamic_slice(both, index, (1, 1, rows, 3 * cols))[0, 0]

    return block


def edges(block):
    count = 1
    for axis in TILE:
        count *= lax.axis_size(axis)
    forward = [(i, i + 1) for i in range(count - 1)]
    backward = [(b, a) for a, b in forward]
    low = lax.ppermute(block[:, -1:], TILE, forward)
    high = lax.ppermute(block[:, :1], TILE, backward)
    return low, high


def shift(value, step):
    if step == 0:
        return value
    zeros = jnp.zeros_like(value[:, :, :1])
    if step > 0:
        return jnp.concatenate([value[:, :, 1:], zeros], axis=2)
    return jnp.concatenate([zeros, value[:, :, :-1]], axis=2)


def compute(
    acts,
    spatial_weight,
    temporal_weight,
    readout_weight,
    readout_bias,
    tile_of,
    row_of,
    column_of,
    spikes,
):
    fsdp = lax.axis_index("fsdp")
    block = blocks_of(spatial_weight, temporal_weight)
    frames_in = acts[0, 0]
    frames, rows, width, channels = frames_in.shape
    half = channels // 2
    cells = rows * width
    tile_count = lax.axis_size("z") * lax.axis_size("x") * lax.axis_size("core")
    rep_count = lax.axis_size("fsdp")
    neurons = readout_weight.shape[1]
    capacity = max(2, 5 * neurons // (2 * tile_count))
    slot_count = tile_count * capacity
    scale_factor = 1.0 / (rep_count * frames)
    low, high = edges(frames_in)

    def local(value):
        return jnp.where(
            fsdp == 0, value, jnp.concatenate([value[:, half:], value[:, :half]], axis=1)
        )

    tile_ids = tile_of[0, :, 0]
    cell_ids = row_of[0] * width + column_of[0]
    same_tile = tile_ids[:, None] == tile_ids[None, :]
    order = jnp.arange(neurons)
    rank_ids = jnp.sum((same_tile & (order[None, :] < order[:, None])).astype(jnp.int32), axis=1)
    slot_ids = tile_ids * capacity + rank_ids
    selector = (slot_ids[None, :] == jnp.arange(slot_count)[:, None]).astype(BF)
    table = jnp.concatenate(
        [
            local(readout_weight[0]),
            readout_bias[0][:, None],
            cell_ids.astype(BF)[:, None],
            jnp.ones((neurons, 1), BF),
            spikes[0, 0].T.astype(BF),
            jnp.zeros((neurons, PACK - channels - 3 - frames), BF),
        ],
        axis=1,
    )
    packed = jnp.dot(selector, table, preferred_element_type=F32).astype(BF)
    held = lax.all_to_all(
        packed.reshape(tile_count, capacity, PACK),
        TILE,
        split_axis=0,
        concat_axis=0,
        tiled=True,
    ).reshape(slot_count, PACK)
    slot_weight = held[:, :channels]
    extras = held[:, channels : channels + 3 + frames].astype(F32)
    slot_bias = extras[:, 0]
    slot_cell = jnp.where(extras[:, 2] > 0.5, extras[:, 1].astype(jnp.int32), cells)
    slot_spikes = extras[:, 3:].T

    shifted_rows = [
        jnp.concatenate([low, frames_in[:, :1]], axis=1).reshape(-1, channels),
        frames_in.reshape(-1, channels),
        jnp.concatenate([frames_in[:, 1:], high], axis=1).reshape(-1, channels),
    ]
    taller = jnp.concatenate(shifted_rows, axis=1)

    def convolve(weights):
        sums = jnp.dot(taller, weights, preferred_element_type=F32)
        sums = sums.reshape(frames, rows, width, 3 * half)
        total = (
            shift(sums[..., :half], -1)
            + sums[..., half : 2 * half]
            + shift(sums[..., 2 * half :], 1)
        )
        return total.astype(BF).reshape(frames, cells, half)

    near_weights = jnp.concatenate(
        [
            jnp.concatenate([spatial_weight[3 * a + b] for b in range(3)], axis=1)
            for a in range(3)
        ]
    )
    near_out = convolve(near_weights)
    far_out = convolve(jnp.concatenate([block(h, g) for g in range(3) for h in range(2)]))
    spatial_out = jnp.concatenate([near_out, far_out], axis=2)

    lag_blocks = [block(q ^ fsdp, 3) for q in range(2)]
    temporal = [
        jnp.concatenate(
            [
                jnp.concatenate(
                    [
                        lax.dynamic_slice_in_dim(temporal_weight[lag], (q ^ fsdp) * half, half, 0),
                        lag_blocks[q][:, lag * half : (lag + 1) * half],
                    ],
                    axis=1,
                )
                for q in range(2)
            ]
        )
        for lag in range(3)
    ]
    causal = jnp.pad(spatial_out, ((2, 0), (0, 0), (0, 0)))
    mixed = jnp.zeros((frames * cells, channels), F32)
    for lag in range(3):
        mixed = mixed + jnp.dot(
            causal[2 - lag : 2 - lag + frames].reshape(-1, channels),
            temporal[lag],
            preferred_element_type=F32,
        )
    features = jax.nn.elu(mixed).astype(BF)

    here = jnp.arange(cells)[:, None] == slot_cell[None, :]
    scores = lax.dot_general(
        features, slot_weight, (((1,), (1,)), ((), ())), preferred_element_type=F32
    ).reshape(frames, cells, slot_count)
    logits = jnp.sum(jnp.where(here[None], scores, 0.0), axis=1) + slot_bias[None, :]
    delta = (jnp.exp(logits) - slot_spikes) * scale_factor
    coarse = lax.reduce_precision(delta, 8, 7)
    pieces = jnp.concatenate([coarse, delta - coarse], axis=1).astype(BF)
    here_twice = jnp.concatenate([here, here], axis=1)
    spread_twice = jnp.where(here_twice[None], pieces[:, None, :], jnp.zeros((), BF)).reshape(
        -1, 2 * slot_count
    )
    spread = spread_twice[:, :slot_count]
    feature_grad = jnp.dot(
        spread_twice,
        jnp.concatenate([slot_weight, slot_weight]),
        preferred_element_type=F32,
    )
    slope = jnp.where(mixed > 0, 1.0, jnp.exp(jnp.minimum(mixed, 0.0)))
    mixed_grad = (feature_grad * slope).astype(BF)
    back_pad = jnp.pad(mixed_grad.reshape(frames, cells, channels), ((0, 2), (0, 0), (0, 0)))
    later = jnp.concatenate(
        [back_pad[lag : lag + frames].reshape(-1, channels) for lag in range(3)], axis=1
    )
    grad_t = contract_rows(spatial_out.reshape(-1, channels), later)
    slot_grad = contract_rows(spread, features)
    slot_bias_grad = jnp.sum(delta, axis=0)
    back = jnp.concatenate(
        [slot_grad, slot_bias_grad[:, None], jnp.zeros((slot_count, PACK - channels - 1), F32)],
        axis=1,
    ).astype(BF)
    back = lax.optimization_barrier(back)

    spatial_back = lax.dot_general(
        later,
        jnp.concatenate(temporal, axis=1),
        (((1,), (1,)), ((), ())),
        preferred_element_type=F32,
    )
    spatial_back = spatial_back.reshape(frames, rows, width, channels)
    wider = jnp.concatenate(
        [shift(spatial_back, 1 - b).astype(BF).reshape(-1, channels) for b in range(3)], axis=1
    )
    grad_0 = contract_rows(shifted_rows[0], wider)
    first_part = reduce_first((grad_t, grad_0), (fsdp, 0))
    grad_1 = contract_rows(shifted_rows[1], wider)
    first_part, wider = lax.optimization_barrier((first_part, wider))
    grad_2 = contract_rows(shifted_rows[2], wider)
    second_part = reduce_first((grad_1, grad_2), (0, 0))
    total_1 = reduce_rest("s1", first_part)
    total_2 = reduce_rest("s2", second_part)

    returned = lax.all_to_all(
        back.reshape(tile_count, capacity, PACK), TILE, split_axis=0, concat_axis=0, tiled=True
    ).reshape(slot_count, PACK)
    mine = contract_rows(selector, returned)
    mine = jnp.concatenate([local(mine[:, :channels]), mine[:, channels:]], axis=1).astype(BF)
    other = lax.ppermute(mine, "fsdp", [(0, 1), (1, 0)])
    summed = mine.astype(F32) + other.astype(F32)
    weight_grad = summed[:, :channels]
    bias_grad = summed[:, channels]

    def taps(value):
        return [value[:, b * half : (b + 1) * half].astype(F32) for b in range(3)]

    total_temporal = jnp.stack(taps(total_1[0]))
    total_spatial = jnp.stack(taps(total_1[1]) + taps(total_2[0]) + taps(total_2[1]))
    return (total_spatial, total_temporal, weight_grad[None], bias_grad[None])


def solution(mesh):
    shape = mesh.devices.shape
    split = Mesh(
        mesh.devices.reshape(shape[0], 4, 4, 2, shape[2]), ("fsdp", "z", "x", "core", "scan")
    )
    return jax.shard_map(
        compute,
        mesh=split,
        in_specs=(
            P("scan", "fsdp", None, TILE, None, None),
            P(None, None, "fsdp"),
            P(None, None, "fsdp"),
            P("scan", TILE, None),
            P("scan", TILE),
            P("scan", TILE, None),
            P("scan", TILE),
            P("scan", TILE),
            P("scan", "fsdp", None, TILE),
        ),
        out_specs=(
            P(None, None, "fsdp"),
            P(None, None, "fsdp"),
            P("scan", TILE, None),
            P("scan", TILE),
        ),
        check_vma=False,
    )
```

```python
import math

import jax
import jax.numpy as jnp
from jax import lax
from jax.sharding import Mesh, PartitionSpec as P


BF = jnp.bfloat16
F32 = jnp.float32
TILE = ("z", "x", "core")
ALL = ("fsdp", "z", "x", "core", "scan")
PACK = 640


def contract_rows(left, right):
    return lax.dot_general(left, right, (((0,), (0,)), ((), ())), preferred_element_type=F32)


def swap(value, axis, kind):
    if axis == "core":
        pairs = ((0, 1),)
    elif kind == 0:
        pairs = ((0, 1), (2, 3))
    else:
        pairs = ((1, 2), (3, 0))
    name = ("fsdp", "scan") if axis == "y" else axis
    perm = [pair for a, b in pairs for pair in ((a, b), (b, a))]
    return lax.ppermute(value, name, perm)


def bit(axis, kind):
    if axis == "core":
        return lax.axis_index("core")
    if axis == "y":
        place = lax.axis_index("fsdp") * 2 + lax.axis_index("scan")
    else:
        place = lax.axis_index(axis)
    return place >> 1 if kind else (place ^ (place >> 1)) & 1


def permute_by_core(value, axes, flip):
    sizes = [lax.axis_size(name) for name in ALL]
    perm = []
    for index in range(math.prod(sizes)):
        rest, spot = index, {}
        for name, size in zip(reversed(ALL), reversed(sizes)):
            spot[name] = rest % size
            rest //= size
        spot["y"] = spot["fsdp"] * 2 + spot["scan"]
        spot[axes[spot["core"]]] ^= flip
        spot["fsdp"], spot["scan"] = spot["y"] // 2, spot["y"] % 2
        target = 0
        for name, size in zip(ALL, sizes):
            target = target * size + spot[name]
        perm.append((index, target))
    return lax.ppermute(value, ALL, perm)


def place_by_core(axes):
    first, second = (lax.axis_index(axis) for axis in axes)
    return jnp.where(lax.axis_index("core") == 0, first, second)


def quarter(value, axes):
    size = value.shape[1] // 4
    mine = place_by_core(axes)
    total = lax.dynamic_slice_in_dim(value, mine * size, size, 1)
    for flip in (1, 3, 2):
        sent = lax.dynamic_slice_in_dim(value, (mine ^ flip) * size, size, 1)
        total = total + permute_by_core(sent.astype(BF), axes, flip).astype(F32)
    return total


def sum_columns(value):
    cols = value.shape[2] // 6
    own, far = (
        jnp.concatenate([value[:, :, (2 * g + h) * cols :][:, :, :cols] for g in range(3)], axis=2)
        for h in range(2)
    )
    own, far = own.astype(BF), far.astype(BF)
    near = permute_by_core(own, ("y", "y"), 1)
    across = permute_by_core(far, ("y", "y"), 3)
    opposite = permute_by_core(far, ("y", "y"), 2)
    return (own.astype(F32) + near.astype(F32)) + (across.astype(F32) + opposite.astype(F32))


def regather(value, axes):
    mine = place_by_core(axes)
    got = [value] + [permute_by_core(value, axes, flip) for flip in (1, 2, 3)]
    pieces = []
    for spot in range(4):
        flip = mine ^ spot
        pieces.append(
            jnp.where(
                flip < 2,
                jnp.where(flip == 0, got[0], got[1]),
                jnp.where(flip == 2, got[2], got[3]),
            )
        )
    return jnp.concatenate(pieces, axis=1)


def joined(value, other, mine):
    first = mine == 0
    return jnp.concatenate(
        [jnp.where(first, value, other), jnp.where(first, other, value)], axis=1
    )


def reduce_first(grads, flips):
    core = lax.axis_index("core")
    size = grads[0].shape[0] // 2
    kept, sent = (
        jnp.stack(
            [
                lax.dynamic_slice_in_dim(grad, (core ^ flip ^ far) * size, size, 0)
                for grad, flip in zip(grads, flips)
            ]
        )
        for far in range(2)
    )
    return kept + swap(sent.astype(BF), "core", 0).astype(F32)


def reduce_middle(value):
    value = quarter(value, ("x", "z"))
    value = quarter(value, ("z", "x"))
    return sum_columns(value).astype(BF)


def reduce_last(value):
    value = regather(value, ("z", "x"))
    value = regather(value, ("x", "z"))
    return joined(value, swap(value, "core", 0), lax.axis_index("core"))


def blocks_of(spatial, temporal):
    color = bit("z", 0) ^ (bit("z", 1) * 2) ^ (bit("y", 0) * 3)
    rows, cols = spatial.shape[1] // 2, spatial.shape[2]
    core = lax.axis_index("core")
    start = core * rows
    taps = lax.dynamic_slice(spatial, (3 * jnp.minimum(color, 2), start, 0), (3, rows, cols))
    lags = lax.dynamic_slice_in_dim(temporal, start, rows, 1)
    part = jnp.where(color == 3, lags, taps)
    part = jnp.concatenate([part[0], part[1], part[2]], axis=1)
    part = swap(part, "y", 1)
    parts = [part, swap(part, "z", 0), swap(part, "z", 1), swap(part, "y", 0)]
    mine = jnp.stack(parts)
    other = swap(mine, "core", 0)
    both = jnp.stack([mine, other])

    def block(half, group):
        index = (half ^ core, group ^ color, 0, 0)
        return lax.dynamic_slice(both, index, (1, 1, rows, 3 * cols))[0, 0]

    return block


def edges(block):
    count = 1
    for axis in TILE:
        count *= lax.axis_size(axis)
    forward = [(i, i + 1) for i in range(count - 1)]
    backward = [(b, a) for a, b in forward]
    low = lax.ppermute(block[:, -1:], TILE, forward)
    high = lax.ppermute(block[:, :1], TILE, backward)
    return low, high


def shift(value, step):
    if step == 0:
        return value
    zeros = jnp.zeros_like(value[:, :, :1])
    if step > 0:
        return jnp.concatenate([value[:, :, 1:], zeros], axis=2)
    return jnp.concatenate([zeros, value[:, :, :-1]], axis=2)


def compute(
    acts,
    spatial_weight,
    temporal_weight,
    readout_weight,
    readout_bias,
    tile_of,
    row_of,
    column_of,
    spikes,
):
    fsdp = lax.axis_index("fsdp")
    block = blocks_of(spatial_weight, temporal_weight)
    frames_in = acts[0, 0]
    frames, rows, width, channels = frames_in.shape
    half = channels // 2
    cells = rows * width
    tile_count = lax.axis_size("z") * lax.axis_size("x") * lax.axis_size("core")
    rep_count = lax.axis_size("fsdp")
    neurons = readout_weight.shape[1]
    capacity = max(2, 5 * neurons // (2 * tile_count))
    slot_count = tile_count * capacity
    scale_factor = 1.0 / (rep_count * frames)
    low, high = edges(frames_in)

    def local(value):
        return jnp.where(
            fsdp == 0, value, jnp.concatenate([value[:, half:], value[:, :half]], axis=1)
        )

    tile_ids = tile_of[0, :, 0]
    cell_ids = row_of[0] * width + column_of[0]
    same_tile = tile_ids[:, None] == tile_ids[None, :]
    order = jnp.arange(neurons)
    rank_ids = jnp.sum((same_tile & (order[None, :] < order[:, None])).astype(jnp.int32), axis=1)
    slot_ids = tile_ids * capacity + rank_ids
    selector = (slot_ids[None, :] == jnp.arange(slot_count)[:, None]).astype(BF)
    table = jnp.concatenate(
        [
            local(readout_weight[0]),
            readout_bias[0][:, None],
            cell_ids.astype(BF)[:, None],
            jnp.ones((neurons, 1), BF),
            spikes[0, 0].T.astype(BF),
            jnp.zeros((neurons, PACK - channels - 3 - frames), BF),
        ],
        axis=1,
    )
    packed = jnp.dot(selector, table, preferred_element_type=F32).astype(BF)
    held = lax.all_to_all(
        packed.reshape(tile_count, capacity, PACK),
        TILE,
        split_axis=0,
        concat_axis=0,
        tiled=True,
    ).reshape(slot_count, PACK)
    shifted_rows = [
        jnp.concatenate([low, frames_in[:, :1]], axis=1).reshape(-1, channels),
        frames_in.reshape(-1, channels),
        jnp.concatenate([frames_in[:, 1:], high], axis=1).reshape(-1, channels),
    ]
    taller = jnp.concatenate(shifted_rows, axis=1)

    def convolve(weights):
        sums = jnp.dot(taller, weights, preferred_element_type=F32)
        sums = sums.reshape(frames, rows, width, 3 * half)
        total = (
            shift(sums[..., :half], -1)
            + sums[..., half : 2 * half]
            + shift(sums[..., 2 * half :], 1)
        )
        return total.astype(BF).reshape(frames, cells, half)

    near_weights = jnp.concatenate(
        [
            jnp.concatenate([spatial_weight[3 * a + b] for b in range(3)], axis=1)
            for a in range(3)
        ]
    )
    near_out = convolve(near_weights)
    far_out = convolve(jnp.concatenate([block(h, g) for g in range(3) for h in range(2)]))
    far_out, held = lax.optimization_barrier((far_out, held))
    spatial_out = jnp.concatenate([near_out, far_out], axis=2)
    slot_weight = held[:, :channels]
    extras = held[:, channels : channels + 3 + frames].astype(F32)
    slot_bias = extras[:, :1]
    slot_cell = jnp.where(extras[:, 2:3] > 0.5, extras[:, 1:2].astype(jnp.int32), cells)
    slot_spikes = extras[:, 3:]

    lag_blocks = [block(q ^ fsdp, 3) for q in range(2)]
    temporal = [
        jnp.concatenate(
            [
                jnp.concatenate(
                    [
                        lax.dynamic_slice_in_dim(temporal_weight[lag], (q ^ fsdp) * half, half, 0),
                        lag_blocks[q][:, lag * half : (lag + 1) * half],
                    ],
                    axis=1,
                )
                for q in range(2)
            ]
        )
        for lag in range(3)
    ]
    causal = jnp.pad(spatial_out, ((2, 0), (0, 0), (0, 0)))
    mixed = jnp.zeros((frames * cells, channels), F32)
    for lag in range(3):
        mixed = mixed + jnp.dot(
            causal[2 - lag : 2 - lag + frames].reshape(-1, channels),
            temporal[lag],
            preferred_element_type=F32,
        )
    features = jax.nn.elu(mixed).astype(BF)

    here = slot_cell == jnp.arange(cells)[None, :]
    scores = lax.dot_general(
        slot_weight, features, (((1,), (1,)), ((), ())), preferred_element_type=F32
    ).reshape(slot_count, frames, cells)
    logits = jnp.sum(jnp.where(here[:, None, :], scores, 0.0), axis=2) + slot_bias
    delta = (jnp.exp(logits) - slot_spikes) * scale_factor
    coarse = lax.reduce_precision(delta, 8, 7)
    spread, rest = (
        jnp.where(here[:, None, :], piece.astype(BF)[:, :, None], jnp.zeros((), BF)).reshape(
            slot_count, -1
        )
        for piece in (coarse, delta - coarse)
    )
    feature_grad = contract_rows(
        jnp.concatenate([spread, rest]), jnp.concatenate([slot_weight, slot_weight])
    )
    slope = jnp.where(mixed > 0, 1.0, jnp.exp(jnp.minimum(mixed, 0.0)))
    mixed_grad = (feature_grad * slope).astype(BF)
    back_pad = jnp.pad(mixed_grad.reshape(frames, cells, channels), ((0, 2), (0, 0), (0, 0)))
    later = jnp.concatenate(
        [back_pad[lag : lag + frames].reshape(-1, channels) for lag in range(3)], axis=1
    )
    grad_t = contract_rows(spatial_out.reshape(-1, channels), later)
    slot_grad = jnp.dot(spread, features, preferred_element_type=F32)
    slot_bias_grad = jnp.sum(delta, axis=1, keepdims=True)
    back = jnp.concatenate(
        [slot_grad, slot_bias_grad, jnp.zeros((slot_count, PACK - channels - 1), F32)],
        axis=1,
    ).astype(BF)
    back = lax.optimization_barrier(back)

    spatial_back = lax.dot_general(
        later,
        jnp.concatenate(temporal, axis=1),
        (((1,), (1,)), ((), ())),
        preferred_element_type=F32,
    )
    spatial_back = spatial_back.reshape(frames, rows, width, channels)
    wider = jnp.concatenate(
        [shift(spatial_back, 1 - b).astype(BF).reshape(-1, channels) for b in range(3)], axis=1
    )
    grad_0 = contract_rows(shifted_rows[0], wider)
    first_part = reduce_first((grad_t, grad_0), (fsdp, 0))
    grad_1 = contract_rows(shifted_rows[1], wider)
    first_part, wider = lax.optimization_barrier((first_part, wider))
    grad_2 = contract_rows(shifted_rows[2], wider)
    second_part = reduce_first((grad_1, grad_2), (0, 0))
    middle_1 = reduce_middle(first_part)
    middle_2 = reduce_middle(second_part)

    returned = lax.all_to_all(
        back.reshape(tile_count, capacity, PACK), TILE, split_axis=0, concat_axis=0, tiled=True
    ).reshape(slot_count, PACK)
    returned, middle_2 = lax.optimization_barrier((returned, middle_2))
    mine = contract_rows(selector, returned)
    mine = jnp.concatenate([local(mine[:, :channels]), mine[:, channels:]], axis=1).astype(BF)
    other = lax.ppermute(mine, "fsdp", [(0, 1), (1, 0)])
    total_1 = reduce_last(middle_1)
    total_2 = reduce_last(middle_2)
    summed = mine.astype(F32) + other.astype(F32)
    weight_grad = summed[:, :channels]
    bias_grad = summed[:, channels]

    def taps(value):
        return [value[:, b * half : (b + 1) * half].astype(F32) for b in range(3)]

    total_temporal = jnp.stack(taps(total_1[0]))
    total_spatial = jnp.stack(taps(total_1[1]) + taps(total_2[0]) + taps(total_2[1]))
    return (total_spatial, total_temporal, weight_grad[None], bias_grad[None])


def solution(mesh):
    shape = mesh.devices.shape
    split = Mesh(
        mesh.devices.reshape(shape[0], 4, 4, 2, shape[2]), ("fsdp", "z", "x", "core", "scan")
    )
    return jax.shard_map(
        compute,
        mesh=split,
        in_specs=(
            P("scan", "fsdp", None, TILE, None, None),
            P(None, None, "fsdp"),
            P(None, None, "fsdp"),
            P("scan", TILE, None),
            P("scan", TILE),
            P("scan", TILE, None),
            P("scan", TILE),
            P("scan", TILE),
            P("scan", "fsdp", None, TILE),
        ),
        out_specs=(
            P(None, None, "fsdp"),
            P(None, None, "fsdp"),
            P("scan", TILE, None),
            P("scan", TILE),
        ),
        check_vma=False,
    )
```

```python
import math

import jax
import jax.numpy as jnp
from jax import lax
from jax.sharding import Mesh, PartitionSpec as P


BF = jnp.bfloat16
F32 = jnp.float32
TILE = ("z", "x", "core")
ALL = ("fsdp", "z", "x", "core", "scan")
PACK = 640


def contract_rows(left, right):
    return lax.dot_general(left, right, (((0,), (0,)), ((), ())), preferred_element_type=F32)


def swap(value, axis, kind):
    if axis == "core":
        pairs = ((0, 1),)
    elif kind == 0:
        pairs = ((0, 1), (2, 3))
    else:
        pairs = ((1, 2), (3, 0))
    name = ("fsdp", "scan") if axis == "y" else axis
    perm = [pair for a, b in pairs for pair in ((a, b), (b, a))]
    return lax.ppermute(value, name, perm)


def bit(axis, kind):
    if axis == "core":
        return lax.axis_index("core")
    if axis == "y":
        place = lax.axis_index("fsdp") * 2 + lax.axis_index("scan")
    else:
        place = lax.axis_index(axis)
    return place >> 1 if kind else (place ^ (place >> 1)) & 1


def permute_by_core(value, axes, flip):
    sizes = [lax.axis_size(name) for name in ALL]
    perm = []
    for index in range(math.prod(sizes)):
        rest, spot = index, {}
        for name, size in zip(reversed(ALL), reversed(sizes)):
            spot[name] = rest % size
            rest //= size
        spot["y"] = spot["fsdp"] * 2 + spot["scan"]
        spot[axes[spot["core"]]] ^= flip
        spot["fsdp"], spot["scan"] = spot["y"] // 2, spot["y"] % 2
        target = 0
        for name, size in zip(ALL, sizes):
            target = target * size + spot[name]
        perm.append((index, target))
    return lax.ppermute(value, ALL, perm)


def place_by_core(axes):
    first, second = (lax.axis_index(axis) for axis in axes)
    return jnp.where(lax.axis_index("core") == 0, first, second)


def quarter(value, axes):
    size = value.shape[1] // 4
    mine = place_by_core(axes)
    total = lax.dynamic_slice_in_dim(value, mine * size, size, 1)
    for flip in (1, 3, 2):
        sent = lax.dynamic_slice_in_dim(value, (mine ^ flip) * size, size, 1)
        total = total + permute_by_core(sent.astype(BF), axes, flip).astype(F32)
    return total


def sum_columns(value):
    cols = value.shape[2] // 6
    own, far = (
        jnp.concatenate([value[:, :, (2 * g + h) * cols :][:, :, :cols] for g in range(3)], axis=2)
        for h in range(2)
    )
    own, far = own.astype(BF), far.astype(BF)
    near = permute_by_core(own, ("y", "y"), 1)
    across = permute_by_core(far, ("y", "y"), 3)
    opposite = permute_by_core(far, ("y", "y"), 2)
    return (own.astype(F32) + near.astype(F32)) + (across.astype(F32) + opposite.astype(F32))


def regather(value, axes):
    mine = place_by_core(axes)
    got = [value] + [permute_by_core(value, axes, flip) for flip in (1, 2, 3)]
    pieces = []
    for spot in range(4):
        flip = mine ^ spot
        pieces.append(
            jnp.where(
                flip < 2,
                jnp.where(flip == 0, got[0], got[1]),
                jnp.where(flip == 2, got[2], got[3]),
            )
        )
    return jnp.concatenate(pieces, axis=1)


def joined(value, other, mine):
    first = mine == 0
    return jnp.concatenate(
        [jnp.where(first, value, other), jnp.where(first, other, value)], axis=1
    )


def reduce_first(grads, flips):
    core = lax.axis_index("core")
    size = grads[0].shape[0] // 2
    kept, sent = (
        jnp.stack(
            [
                lax.dynamic_slice_in_dim(grad, (core ^ flip ^ far) * size, size, 0)
                for grad, flip in zip(grads, flips)
            ]
        )
        for far in range(2)
    )
    return kept + swap(sent.astype(BF), "core", 0).astype(F32)


def reduce_rows(value):
    return quarter(value, ("x", "z"))


def reduce_middle(value):
    value = quarter(value, ("z", "x"))
    return sum_columns(value).astype(BF)


def reduce_last(value):
    value = regather(value, ("z", "x"))
    value = regather(value, ("x", "z"))
    return joined(value, swap(value, "core", 0), lax.axis_index("core"))


def blocks_of(spatial, temporal):
    color = bit("z", 0) ^ (bit("z", 1) * 2) ^ (bit("y", 0) * 3)
    rows, cols = spatial.shape[1] // 2, spatial.shape[2]
    core = lax.axis_index("core")
    start = core * rows
    taps = lax.dynamic_slice(spatial, (3 * jnp.minimum(color, 2), start, 0), (3, rows, cols))
    lags = lax.dynamic_slice_in_dim(temporal, start, rows, 1)
    part = jnp.where(color == 3, lags, taps)
    part = jnp.concatenate([part[0], part[1], part[2]], axis=1)
    part = swap(part, "y", 1)
    parts = [part, swap(part, "z", 0), swap(part, "z", 1), swap(part, "y", 0)]
    mine = jnp.stack(parts)
    other = swap(mine, "core", 0)
    both = jnp.stack([mine, other])

    def block(half, group):
        index = (half ^ core, group ^ color, 0, 0)
        return lax.dynamic_slice(both, index, (1, 1, rows, 3 * cols))[0, 0]

    return block


def edges(block):
    count = 1
    for axis in TILE:
        count *= lax.axis_size(axis)
    forward = [(i, i + 1) for i in range(count - 1)]
    backward = [(b, a) for a, b in forward]
    low = lax.ppermute(block[:, -1:], TILE, forward)
    high = lax.ppermute(block[:, :1], TILE, backward)
    return low, high


def shift(value, step):
    if step == 0:
        return value
    zeros = jnp.zeros_like(value[:, :, :1])
    if step > 0:
        return jnp.concatenate([value[:, :, 1:], zeros], axis=2)
    return jnp.concatenate([zeros, value[:, :, :-1]], axis=2)


def compute(
    acts,
    spatial_weight,
    temporal_weight,
    readout_weight,
    readout_bias,
    tile_of,
    row_of,
    column_of,
    spikes,
):
    fsdp = lax.axis_index("fsdp")
    block = blocks_of(spatial_weight, temporal_weight)
    frames_in = acts[0, 0]
    frames, rows, width, channels = frames_in.shape
    half = channels // 2
    cells = rows * width
    tile_count = lax.axis_size("z") * lax.axis_size("x") * lax.axis_size("core")
    rep_count = lax.axis_size("fsdp")
    neurons = readout_weight.shape[1]
    capacity = max(2, 5 * neurons // (2 * tile_count))
    slot_count = tile_count * capacity
    scale_factor = 1.0 / (rep_count * frames)
    low, high = edges(frames_in)

    def local(value):
        return jnp.where(
            fsdp == 0, value, jnp.concatenate([value[:, half:], value[:, :half]], axis=1)
        )

    tile_ids = tile_of[0, :, 0]
    cell_ids = row_of[0] * width + column_of[0]
    same_tile = tile_ids[:, None] == tile_ids[None, :]
    order = jnp.arange(neurons)
    rank_ids = jnp.sum((same_tile & (order[None, :] < order[:, None])).astype(jnp.int32), axis=1)
    slot_ids = tile_ids * capacity + rank_ids
    selector = (slot_ids[None, :] == jnp.arange(slot_count)[:, None]).astype(BF)
    table = jnp.concatenate(
        [
            local(readout_weight[0]),
            readout_bias[0][:, None],
            cell_ids.astype(BF)[:, None],
            jnp.ones((neurons, 1), BF),
            spikes[0, 0].T.astype(BF),
            jnp.zeros((neurons, PACK - channels - 3 - frames), BF),
        ],
        axis=1,
    )
    packed = jnp.dot(selector, table, preferred_element_type=F32).astype(BF)
    held = lax.all_to_all(
        packed.reshape(tile_count, capacity, PACK),
        TILE,
        split_axis=0,
        concat_axis=0,
        tiled=True,
    ).reshape(slot_count, PACK)
    shifted_rows = [
        jnp.concatenate([low, frames_in[:, :1]], axis=1).reshape(-1, channels),
        frames_in.reshape(-1, channels),
        jnp.concatenate([frames_in[:, 1:], high], axis=1).reshape(-1, channels),
    ]
    taller = jnp.concatenate(shifted_rows, axis=1)

    def convolve(weights):
        sums = jnp.dot(taller, weights, preferred_element_type=F32)
        sums = sums.reshape(frames, rows, width, 3 * half)
        total = (
            shift(sums[..., :half], -1)
            + sums[..., half : 2 * half]
            + shift(sums[..., 2 * half :], 1)
        )
        return total.astype(BF).reshape(frames, cells, half)

    near_weights = jnp.concatenate(
        [
            jnp.concatenate([spatial_weight[3 * a + b] for b in range(3)], axis=1)
            for a in range(3)
        ]
    )
    near_out = convolve(near_weights)
    far_out = convolve(jnp.concatenate([block(h, g) for g in range(3) for h in range(2)]))
    far_out, held = lax.optimization_barrier((far_out, held))
    spatial_out = jnp.concatenate([near_out, far_out], axis=2)
    slot_weight = held[:, :channels]
    extras = held[:, channels : channels + 3 + frames].astype(F32)
    slot_bias = extras[:, :1]
    slot_cell = jnp.where(extras[:, 2:3] > 0.5, extras[:, 1:2].astype(jnp.int32), cells)
    slot_spikes = extras[:, 3:]

    lag_blocks = [block(q ^ fsdp, 3) for q in range(2)]
    temporal = [
        jnp.concatenate(
            [
                jnp.concatenate(
                    [
                        lax.dynamic_slice_in_dim(temporal_weight[lag], (q ^ fsdp) * half, half, 0),
                        lag_blocks[q][:, lag * half : (lag + 1) * half],
                    ],
                    axis=1,
                )
                for q in range(2)
            ]
        )
        for lag in range(3)
    ]
    causal = jnp.pad(spatial_out, ((2, 0), (0, 0), (0, 0)))
    mixed = jnp.zeros((frames * cells, channels), F32)
    for lag in range(3):
        mixed = mixed + jnp.dot(
            causal[2 - lag : 2 - lag + frames].reshape(-1, channels),
            temporal[lag],
            preferred_element_type=F32,
        )
    features = jax.nn.elu(mixed).astype(BF)

    here = slot_cell == jnp.arange(cells)[None, :]
    scores = lax.dot_general(
        slot_weight, features, (((1,), (1,)), ((), ())), preferred_element_type=F32
    ).reshape(slot_count, frames, cells)
    logits = jnp.sum(jnp.where(here[:, None, :], scores, 0.0), axis=2) + slot_bias
    delta = (jnp.exp(logits) - slot_spikes) * scale_factor
    coarse = lax.reduce_precision(delta, 8, 7)
    spread, rest = (
        jnp.where(here[:, None, :], piece.astype(BF)[:, :, None], jnp.zeros((), BF)).reshape(
            slot_count, -1
        )
        for piece in (coarse, delta - coarse)
    )
    feature_grad = contract_rows(
        jnp.concatenate([spread, rest]), jnp.concatenate([slot_weight, slot_weight])
    )
    slope = jnp.where(mixed > 0, 1.0, jnp.exp(jnp.minimum(mixed, 0.0)))
    mixed_grad = (feature_grad * slope).astype(BF)
    back_pad = jnp.pad(mixed_grad.reshape(frames, cells, channels), ((0, 2), (0, 0), (0, 0)))
    later = jnp.concatenate(
        [back_pad[lag : lag + frames].reshape(-1, channels) for lag in range(3)], axis=1
    )
    grad_t = contract_rows(spatial_out.reshape(-1, channels), later)
    slot_grad = jnp.dot(spread, features, preferred_element_type=F32)
    slot_bias_grad = jnp.sum(delta, axis=1, keepdims=True)
    back = jnp.concatenate(
        [slot_grad, slot_bias_grad, jnp.zeros((slot_count, PACK - channels - 1), F32)],
        axis=1,
    ).astype(BF)
    back = lax.optimization_barrier(back)

    spatial_back = lax.dot_general(
        later,
        jnp.concatenate(temporal, axis=1),
        (((1,), (1,)), ((), ())),
        preferred_element_type=F32,
    )
    spatial_back = spatial_back.reshape(frames, rows, width, channels)
    wider = jnp.concatenate(
        [shift(spatial_back, 1 - b).astype(BF).reshape(-1, channels) for b in range(3)], axis=1
    )
    grad_0 = contract_rows(shifted_rows[0], wider)
    first_part = reduce_first((grad_t, grad_0), (fsdp, 0))
    grad_1 = contract_rows(shifted_rows[1], wider)
    first_part, wider = lax.optimization_barrier((first_part, wider))
    grad_2 = contract_rows(shifted_rows[2], wider)
    second_part = reduce_first((grad_1, grad_2), (0, 0))
    middle = reduce_middle(jnp.concatenate([reduce_rows(first_part), reduce_rows(second_part)]))

    returned = lax.all_to_all(
        back.reshape(tile_count, capacity, PACK), TILE, split_axis=0, concat_axis=0, tiled=True
    ).reshape(slot_count, PACK)
    returned, middle = lax.optimization_barrier((returned, middle))
    mine = contract_rows(selector, returned)
    mine = jnp.concatenate([local(mine[:, :channels]), mine[:, channels:]], axis=1).astype(BF)
    other = lax.ppermute(mine, "fsdp", [(0, 1), (1, 0)])
    total = reduce_last(middle)
    summed = mine.astype(F32) + other.astype(F32)
    weight_grad = summed[:, :channels]
    bias_grad = summed[:, channels]

    def taps(value):
        return [value[:, b * half : (b + 1) * half].astype(F32) for b in range(3)]

    total_temporal = jnp.stack(taps(total[0]))
    total_spatial = jnp.stack(taps(total[1]) + taps(total[2]) + taps(total[3]))
    return (total_spatial, total_temporal, weight_grad[None], bias_grad[None])


def solution(mesh):
    shape = mesh.devices.shape
    split = Mesh(
        mesh.devices.reshape(shape[0], 4, 4, 2, shape[2]), ("fsdp", "z", "x", "core", "scan")
    )
    return jax.shard_map(
        compute,
        mesh=split,
        in_specs=(
            P("scan", "fsdp", None, TILE, None, None),
            P(None, None, "fsdp"),
            P(None, None, "fsdp"),
            P("scan", TILE, None),
            P("scan", TILE),
            P("scan", TILE, None),
            P("scan", TILE),
            P("scan", TILE),
            P("scan", "fsdp", None, TILE),
        ),
        out_specs=(
            P(None, None, "fsdp"),
            P(None, None, "fsdp"),
            P("scan", TILE, None),
            P("scan", TILE),
        ),
        check_vma=False,
    )
```

```python
import math

import jax
import jax.numpy as jnp
from jax import lax
from jax.experimental import pallas as pl
from jax.experimental.pallas import tpu as pltpu
from jax.sharding import Mesh, PartitionSpec as P


BF = jnp.bfloat16
F32 = jnp.float32
TILE = ("z", "x", "core")
ALL = ("fsdp", "z", "x", "core", "scan")
PACK = 640


def contract_rows(left, right):
    return lax.dot_general(left, right, (((0,), (0,)), ((), ())), preferred_element_type=F32)


def swap(value, axis, kind):
    if axis == "core":
        pairs = ((0, 1),)
    elif kind == 0:
        pairs = ((0, 1), (2, 3))
    else:
        pairs = ((1, 2), (3, 0))
    name = ("fsdp", "scan") if axis == "y" else axis
    perm = [pair for a, b in pairs for pair in ((a, b), (b, a))]
    return lax.ppermute(value, name, perm)


def bit(axis, kind):
    if axis == "core":
        return lax.axis_index("core")
    if axis == "y":
        place = lax.axis_index("fsdp") * 2 + lax.axis_index("scan")
    else:
        place = lax.axis_index(axis)
    return place >> 1 if kind else (place ^ (place >> 1)) & 1


def permute_by_core(value, axes, flip):
    sizes = [lax.axis_size(name) for name in ALL]
    perm = []
    for index in range(math.prod(sizes)):
        rest, spot = index, {}
        for name, size in zip(reversed(ALL), reversed(sizes)):
            spot[name] = rest % size
            rest //= size
        spot["y"] = spot["fsdp"] * 2 + spot["scan"]
        spot[axes[spot["core"]]] ^= flip
        spot["fsdp"], spot["scan"] = spot["y"] // 2, spot["y"] % 2
        target = 0
        for name, size in zip(ALL, sizes):
            target = target * size + spot[name]
        perm.append((index, target))
    return lax.ppermute(value, ALL, perm)


def place_by_core(axes):
    first, second = (lax.axis_index(axis) for axis in axes)
    return jnp.where(lax.axis_index("core") == 0, first, second)


def quarter(value, axes):
    size = value.shape[1] // 4
    mine = place_by_core(axes)
    total = lax.dynamic_slice_in_dim(value, mine * size, size, 1)
    for flip in (1, 3, 2):
        sent = lax.dynamic_slice_in_dim(value, (mine ^ flip) * size, size, 1)
        total = total + permute_by_core(sent.astype(BF), axes, flip).astype(F32)
    return total


def sum_columns(value):
    cols = value.shape[2] // 6
    own, far = (
        jnp.concatenate([value[:, :, (2 * g + h) * cols :][:, :, :cols] for g in range(3)], axis=2)
        for h in range(2)
    )
    own, far = own.astype(BF), far.astype(BF)
    near = permute_by_core(own, ("y", "y"), 1)
    across = permute_by_core(far, ("y", "y"), 3)
    opposite = permute_by_core(far, ("y", "y"), 2)
    return (own.astype(F32) + near.astype(F32)) + (across.astype(F32) + opposite.astype(F32))


def regather(value, axes):
    mine = place_by_core(axes)
    got = [value] + [permute_by_core(value, axes, flip) for flip in (1, 2, 3)]
    pieces = []
    for spot in range(4):
        flip = mine ^ spot
        pieces.append(
            jnp.where(
                flip < 2,
                jnp.where(flip == 0, got[0], got[1]),
                jnp.where(flip == 2, got[2], got[3]),
            )
        )
    return jnp.concatenate(pieces, axis=1)


def joined(value, other, mine):
    first = mine == 0
    return jnp.concatenate(
        [jnp.where(first, value, other), jnp.where(first, other, value)], axis=1
    )


def reduce_first(grads, flips):
    core = lax.axis_index("core")
    size = grads[0].shape[0] // 2
    kept, sent = (
        jnp.stack(
            [
                lax.dynamic_slice_in_dim(grad, (core ^ flip ^ far) * size, size, 0)
                for grad, flip in zip(grads, flips)
            ]
        )
        for far in range(2)
    )
    return kept + swap(sent.astype(BF), "core", 0).astype(F32)


def reduce_rows(value):
    return quarter(value, ("x", "z"))


def reduce_middle(value):
    value = quarter(value, ("z", "x"))
    return sum_columns(value).astype(BF)


def reduce_last(value):
    value = regather(value, ("z", "x"))
    value = regather(value, ("x", "z"))
    return joined(value, swap(value, "core", 0), lax.axis_index("core"))


def blocks_of(spatial, temporal):
    color = bit("z", 0) ^ (bit("z", 1) * 2) ^ (bit("y", 0) * 3)
    rows, cols = spatial.shape[1] // 2, spatial.shape[2]
    core = lax.axis_index("core")
    start = core * rows
    taps = lax.dynamic_slice(spatial, (3 * jnp.minimum(color, 2), start, 0), (3, rows, cols))
    lags = lax.dynamic_slice_in_dim(temporal, start, rows, 1)
    part = jnp.where(color == 3, lags, taps)
    part = jnp.concatenate([part[0], part[1], part[2]], axis=1)
    part = swap(part, "y", 1)
    parts = [part, swap(part, "z", 0), swap(part, "z", 1), swap(part, "y", 0)]
    mine = jnp.stack(parts)
    other = swap(mine, "core", 0)
    both = jnp.stack([mine, other])

    def block(half, group):
        index = (half ^ core, group ^ color, 0, 0)
        return lax.dynamic_slice(both, index, (1, 1, rows, 3 * cols))[0, 0]

    return block


def edges(block):
    count = 1
    for axis in TILE:
        count *= lax.axis_size(axis)
    forward = [(i, i + 1) for i in range(count - 1)]
    backward = [(b, a) for a, b in forward]
    low = lax.ppermute(block[:, -1:], TILE, forward)
    high = lax.ppermute(block[:, :1], TILE, backward)
    return low, high


def shift(value, step):
    if step == 0:
        return value
    zeros = jnp.zeros_like(value[:, :, :1])
    if step > 0:
        return jnp.concatenate([value[:, :, 1:], zeros], axis=2)
    return jnp.concatenate([zeros, value[:, :, :-1]], axis=2)


def conv_body(low, block, high, weights, out):
    count, rows, width, channels = block.shape
    top, bottom = block[:, :1], block[:, 1:]
    stacked = (
        jnp.concatenate([low[...], top], axis=1),
        block[...],
        jnp.concatenate([bottom, high[...]], axis=1),
    )
    sums = None
    for a in range(3):
        part = jnp.dot(
            stacked[a].reshape(count * rows * width, channels),
            weights[a * channels : (a + 1) * channels, :],
            preferred_element_type=F32,
        )
        sums = part if sums is None else sums + part
    half = out.shape[2]
    left, middle, right = (sums[:, b * half : (b + 1) * half] for b in range(3))
    column = lax.broadcasted_iota(jnp.int32, left.shape, 0) % width
    size = left.shape[0]
    left = jnp.where(column == 0, 0.0, pltpu.roll(left, 1, 0))
    right = jnp.where(column == width - 1, 0.0, pltpu.roll(right, size - 1, 0))
    out[...] = (left + middle + right).astype(BF).reshape(out.shape)


def convolve(low, block, high, weights):
    frames, rows, width, channels = block.shape
    step = 4
    half = weights.shape[1] // 3

    def edge(count):
        return pl.BlockSpec((step, count, width, channels), lambda i: (i, 0, 0, 0))

    return pl.pallas_call(
        conv_body,
        grid=(frames // step,),
        in_specs=[
            edge(1),
            edge(rows),
            edge(1),
            pl.BlockSpec(weights.shape, lambda i: (0, 0)),
        ],
        out_specs=pl.BlockSpec((step, rows * width, half), lambda i: (i, 0, 0)),
        out_shape=jax.ShapeDtypeStruct((frames, rows * width, half), BF),
        compiler_params=pltpu.CompilerParams(vmem_limit_bytes=32 * 1024 * 1024),
        cost_estimate=pl.CostEstimate(
            flops=2 * frames * rows * width * weights.size,
            bytes_accessed=2 * (block.size * 2 + weights.size + block.size // 2),
            transcendentals=0,
        ),
        name="conv",
    )(low, block, high, weights)


def compute(
    acts,
    spatial_weight,
    temporal_weight,
    readout_weight,
    readout_bias,
    tile_of,
    row_of,
    column_of,
    spikes,
):
    fsdp = lax.axis_index("fsdp")
    block = blocks_of(spatial_weight, temporal_weight)
    frames_in = acts[0, 0]
    frames, rows, width, channels = frames_in.shape
    half = channels // 2
    cells = rows * width
    tile_count = lax.axis_size("z") * lax.axis_size("x") * lax.axis_size("core")
    rep_count = lax.axis_size("fsdp")
    neurons = readout_weight.shape[1]
    capacity = max(2, 5 * neurons // (2 * tile_count))
    slot_count = tile_count * capacity
    scale_factor = 1.0 / (rep_count * frames)
    low, high = edges(frames_in)

    def local(value):
        return jnp.where(
            fsdp == 0, value, jnp.concatenate([value[:, half:], value[:, :half]], axis=1)
        )

    tile_ids = tile_of[0, :, 0]
    cell_ids = row_of[0] * width + column_of[0]
    same_tile = tile_ids[:, None] == tile_ids[None, :]
    order = jnp.arange(neurons)
    rank_ids = jnp.sum((same_tile & (order[None, :] < order[:, None])).astype(jnp.int32), axis=1)
    slot_ids = tile_ids * capacity + rank_ids
    selector = (slot_ids[None, :] == jnp.arange(slot_count)[:, None]).astype(BF)
    table = jnp.concatenate(
        [
            local(readout_weight[0]),
            readout_bias[0][:, None],
            cell_ids.astype(BF)[:, None],
            jnp.ones((neurons, 1), BF),
            spikes[0, 0].T.astype(BF),
            jnp.zeros((neurons, PACK - channels - 3 - frames), BF),
        ],
        axis=1,
    )
    packed = jnp.dot(selector, table, preferred_element_type=F32).astype(BF)
    held = lax.all_to_all(
        packed.reshape(tile_count, capacity, PACK),
        TILE,
        split_axis=0,
        concat_axis=0,
        tiled=True,
    ).reshape(slot_count, PACK)
    shifted_rows = [
        jnp.concatenate([low, frames_in[:, :1]], axis=1).reshape(-1, channels),
        frames_in.reshape(-1, channels),
        jnp.concatenate([frames_in[:, 1:], high], axis=1).reshape(-1, channels),
    ]
    near_weights = jnp.concatenate(
        [
            jnp.concatenate([spatial_weight[3 * a + b] for b in range(3)], axis=1)
            for a in range(3)
        ]
    )
    near_out = convolve(low, frames_in, high, near_weights)
    far_out = convolve(
        low,
        frames_in,
        high,
        jnp.concatenate([block(h, g) for g in range(3) for h in range(2)]),
    )
    far_out, held = lax.optimization_barrier((far_out, held))
    spatial_out = jnp.concatenate([near_out, far_out], axis=2)
    slot_weight = held[:, :channels]
    extras = held[:, channels : channels + 3 + frames].astype(F32)
    slot_bias = extras[:, :1]
    slot_cell = jnp.where(extras[:, 2:3] > 0.5, extras[:, 1:2].astype(jnp.int32), cells)
    slot_spikes = extras[:, 3:]

    lag_blocks = [block(q ^ fsdp, 3) for q in range(2)]
    temporal = [
        jnp.concatenate(
            [
                jnp.concatenate(
                    [
                        lax.dynamic_slice_in_dim(temporal_weight[lag], (q ^ fsdp) * half, half, 0),
                        lag_blocks[q][:, lag * half : (lag + 1) * half],
                    ],
                    axis=1,
                )
                for q in range(2)
            ]
        )
        for lag in range(3)
    ]
    causal = jnp.pad(spatial_out, ((2, 0), (0, 0), (0, 0)))
    mixed = jnp.zeros((frames * cells, channels), F32)
    for lag in range(3):
        mixed = mixed + jnp.dot(
            causal[2 - lag : 2 - lag + frames].reshape(-1, channels),
            temporal[lag],
            preferred_element_type=F32,
        )
    features = jax.nn.elu(mixed).astype(BF)

    here = slot_cell == jnp.arange(cells)[None, :]
    scores = lax.dot_general(
        slot_weight, features, (((1,), (1,)), ((), ())), preferred_element_type=F32
    ).reshape(slot_count, frames, cells)
    logits = jnp.sum(jnp.where(here[:, None, :], scores, 0.0), axis=2) + slot_bias
    delta = (jnp.exp(logits) - slot_spikes) * scale_factor
    coarse = lax.reduce_precision(delta, 8, 7)
    spread, rest = (
        jnp.where(here[:, None, :], piece.astype(BF)[:, :, None], jnp.zeros((), BF)).reshape(
            slot_count, -1
        )
        for piece in (coarse, delta - coarse)
    )
    feature_grad = contract_rows(
        jnp.concatenate([spread, rest]), jnp.concatenate([slot_weight, slot_weight])
    )
    slope = jnp.where(mixed > 0, 1.0, jnp.exp(jnp.minimum(mixed, 0.0)))
    mixed_grad = (feature_grad * slope).astype(BF)
    back_pad = jnp.pad(mixed_grad.reshape(frames, cells, channels), ((0, 2), (0, 0), (0, 0)))
    later = jnp.concatenate(
        [back_pad[lag : lag + frames].reshape(-1, channels) for lag in range(3)], axis=1
    )
    grad_t = contract_rows(spatial_out.reshape(-1, channels), later)
    slot_grad = jnp.dot(spread, features, preferred_element_type=F32)
    slot_bias_grad = jnp.sum(delta, axis=1, keepdims=True)
    back = jnp.concatenate(
        [slot_grad, slot_bias_grad, jnp.zeros((slot_count, PACK - channels - 1), F32)],
        axis=1,
    ).astype(BF)
    back = lax.optimization_barrier(back)

    spatial_back = lax.dot_general(
        later,
        jnp.concatenate(temporal, axis=1),
        (((1,), (1,)), ((), ())),
        preferred_element_type=F32,
    )
    spatial_back = spatial_back.reshape(frames, rows, width, channels)
    wider = jnp.concatenate(
        [shift(spatial_back, 1 - b).astype(BF).reshape(-1, channels) for b in range(3)], axis=1
    )
    grad_0 = contract_rows(shifted_rows[0], wider)
    first_part = reduce_first((grad_t, grad_0), (fsdp, 0))
    grad_1 = contract_rows(shifted_rows[1], wider)
    first_part, wider = lax.optimization_barrier((first_part, wider))
    grad_2 = contract_rows(shifted_rows[2], wider)
    second_part = reduce_first((grad_1, grad_2), (0, 0))
    middle = reduce_middle(jnp.concatenate([reduce_rows(first_part), reduce_rows(second_part)]))

    returned = lax.all_to_all(
        back.reshape(tile_count, capacity, PACK), TILE, split_axis=0, concat_axis=0, tiled=True
    ).reshape(slot_count, PACK)
    returned, middle = lax.optimization_barrier((returned, middle))
    mine = contract_rows(selector, returned)
    mine = jnp.concatenate([local(mine[:, :channels]), mine[:, channels:]], axis=1).astype(BF)
    other = lax.ppermute(mine, "fsdp", [(0, 1), (1, 0)])
    total = reduce_last(middle)
    summed = mine.astype(F32) + other.astype(F32)
    weight_grad = summed[:, :channels]
    bias_grad = summed[:, channels]

    def taps(value):
        return [value[:, b * half : (b + 1) * half].astype(F32) for b in range(3)]

    total_temporal = jnp.stack(taps(total[0]))
    total_spatial = jnp.stack(taps(total[1]) + taps(total[2]) + taps(total[3]))
    return (total_spatial, total_temporal, weight_grad[None], bias_grad[None])


def solution(mesh):
    shape = mesh.devices.shape
    split = Mesh(
        mesh.devices.reshape(shape[0], 4, 4, 2, shape[2]), ("fsdp", "z", "x", "core", "scan")
    )
    return jax.shard_map(
        compute,
        mesh=split,
        in_specs=(
            P("scan", "fsdp", None, TILE, None, None),
            P(None, None, "fsdp"),
            P(None, None, "fsdp"),
            P("scan", TILE, None),
            P("scan", TILE),
            P("scan", TILE, None),
            P("scan", TILE),
            P("scan", TILE),
            P("scan", "fsdp", None, TILE),
        ),
        out_specs=(
            P(None, None, "fsdp"),
            P(None, None, "fsdp"),
            P("scan", TILE, None),
            P("scan", TILE),
        ),
        check_vma=False,
    )
```

```python
import math

import jax
import jax.numpy as jnp
from jax import lax
from jax.experimental import pallas as pl
from jax.experimental.pallas import tpu as pltpu
from jax.sharding import Mesh, PartitionSpec as P


BF = jnp.bfloat16
F32 = jnp.float32
TILE = ("z", "x", "core")
ALL = ("fsdp", "z", "x", "core", "scan")
PACK = 640
CAPACITY = 10
WIDTH = 64


def contract_rows(left, right):
    return lax.dot_general(left, right, (((0,), (0,)), ((), ())), preferred_element_type=F32)


def swap(value, axis, kind):
    if axis == "core":
        pairs = ((0, 1),)
    elif kind == 0:
        pairs = ((0, 1), (2, 3))
    else:
        pairs = ((1, 2), (3, 0))
    name = ("fsdp", "scan") if axis == "y" else axis
    perm = [pair for a, b in pairs for pair in ((a, b), (b, a))]
    return lax.ppermute(value, name, perm)


def bit(axis, kind):
    if axis == "core":
        return lax.axis_index("core")
    if axis == "y":
        place = lax.axis_index("fsdp") * 2 + lax.axis_index("scan")
    else:
        place = lax.axis_index(axis)
    return place >> 1 if kind else (place ^ (place >> 1)) & 1


def permute_by_core(value, axes, flip):
    sizes = [lax.axis_size(name) for name in ALL]
    perm = []
    for index in range(math.prod(sizes)):
        rest, spot = index, {}
        for name, size in zip(reversed(ALL), reversed(sizes)):
            spot[name] = rest % size
            rest //= size
        spot["y"] = spot["fsdp"] * 2 + spot["scan"]
        spot[axes[spot["core"]]] ^= flip
        spot["fsdp"], spot["scan"] = spot["y"] // 2, spot["y"] % 2
        target = 0
        for name, size in zip(ALL, sizes):
            target = target * size + spot[name]
        perm.append((index, target))
    return lax.ppermute(value, ALL, perm)


def place_by_core(axes):
    first, second = (lax.axis_index(axis) for axis in axes)
    return jnp.where(lax.axis_index("core") == 0, first, second)


def quarter(value, axes):
    size = value.shape[1] // 4
    mine = place_by_core(axes)
    total = lax.dynamic_slice_in_dim(value, mine * size, size, 1)
    for flip in (1, 3, 2):
        sent = lax.dynamic_slice_in_dim(value, (mine ^ flip) * size, size, 1)
        total = total + permute_by_core(sent.astype(BF), axes, flip).astype(F32)
    return total


def sum_columns(value):
    cols = value.shape[2] // 6
    own, far = (
        jnp.concatenate([value[:, :, (2 * g + h) * cols :][:, :, :cols] for g in range(3)], axis=2)
        for h in range(2)
    )
    own, far = own.astype(BF), far.astype(BF)
    near = permute_by_core(own, ("y", "y"), 1)
    across = permute_by_core(far, ("y", "y"), 3)
    opposite = permute_by_core(far, ("y", "y"), 2)
    return (own.astype(F32) + near.astype(F32)) + (across.astype(F32) + opposite.astype(F32))


def regather(value, axes):
    mine = place_by_core(axes)
    got = [value] + [permute_by_core(value, axes, flip) for flip in (1, 2, 3)]
    pieces = []
    for spot in range(4):
        flip = mine ^ spot
        pieces.append(
            jnp.where(
                flip < 2,
                jnp.where(flip == 0, got[0], got[1]),
                jnp.where(flip == 2, got[2], got[3]),
            )
        )
    return jnp.concatenate(pieces, axis=1)


def joined(value, other, mine):
    first = mine == 0
    return jnp.concatenate(
        [jnp.where(first, value, other), jnp.where(first, other, value)], axis=1
    )


def reduce_first(grads, flips):
    core = lax.axis_index("core")
    size = grads[0].shape[0] // 2
    kept, sent = (
        jnp.stack(
            [
                lax.dynamic_slice_in_dim(grad, (core ^ flip ^ far) * size, size, 0)
                for grad, flip in zip(grads, flips)
            ]
        )
        for far in range(2)
    )
    return kept + swap(sent.astype(BF), "core", 0).astype(F32)


def reduce_rows(value):
    return quarter(value, ("x", "z"))


def reduce_middle(value):
    value = quarter(value, ("z", "x"))
    return sum_columns(value).astype(BF)


def reduce_last(value):
    value = regather(value, ("z", "x"))
    value = regather(value, ("x", "z"))
    return joined(value, swap(value, "core", 0), lax.axis_index("core"))


def blocks_of(spatial, temporal):
    color = bit("z", 0) ^ (bit("z", 1) * 2) ^ (bit("y", 0) * 3)
    rows, cols = spatial.shape[1] // 2, spatial.shape[2]
    core = lax.axis_index("core")
    start = core * rows
    taps = lax.dynamic_slice(spatial, (3 * jnp.minimum(color, 2), start, 0), (3, rows, cols))
    lags = lax.dynamic_slice_in_dim(temporal, start, rows, 1)
    part = jnp.where(color == 3, lags, taps)
    part = jnp.concatenate([part[0], part[1], part[2]], axis=1)
    part = swap(part, "y", 1)
    parts = [part, swap(part, "z", 0), swap(part, "z", 1), swap(part, "y", 0)]
    mine = jnp.stack(parts)
    other = swap(mine, "core", 0)
    both = jnp.stack([mine, other])

    def block(half, group):
        index = (half ^ core, group ^ color, 0, 0)
        return lax.dynamic_slice(both, index, (1, 1, rows, 3 * cols))[0, 0]

    return block, mine, other, jnp.stack([core, color]).astype(jnp.int32)


def edges(block):
    count = 1
    for axis in TILE:
        count *= lax.axis_size(axis)
    forward = [(i, i + 1) for i in range(count - 1)]
    backward = [(b, a) for a, b in forward]
    low = lax.ppermute(block[:, -1:], TILE, forward)
    high = lax.ppermute(block[:, :1], TILE, backward)
    return low, high


def shift(value, step):
    if step == 0:
        return value
    zeros = jnp.zeros_like(value[:, :, :1])
    if step > 0:
        return jnp.concatenate([value[:, :, 1:], zeros], axis=2)
    return jnp.concatenate([zeros, value[:, :, :-1]], axis=2)


def stacked_rows(low, block, high):
    count, rows, width, channels = block.shape
    parts = (
        jnp.concatenate([low[...], block[:, :1]], axis=1),
        block[...],
        jnp.concatenate([block[:, 1:], high[...]], axis=1),
    )
    return [part.reshape(count * rows * width, channels) for part in parts]


def finish_conv(sums, width, out):
    left, middle, right = sums
    size = left.shape[0]
    column = lax.broadcasted_iota(jnp.int32, left.shape, 0) % width
    left = jnp.where(column == 0, 0.0, pltpu.roll(left, 1, 0))
    right = jnp.where(column == width - 1, 0.0, pltpu.roll(right, size - 1, 0))
    out[...] = (left + middle + right).astype(BF).reshape(out.shape)


def near_body(low, block, high, weights, out):
    stacked = stacked_rows(low, block, high)
    sums = []
    for b in range(3):
        total = None
        for a in range(3):
            part = jnp.dot(stacked[a], weights[3 * a + b], preferred_element_type=F32)
            total = part if total is None else total + part
        sums.append(total)
    finish_conv(sums, block.shape[2], out)


def far_body(place, low, block, high, mine, other, out):
    stacked = stacked_rows(low, block, high)
    core, color = place[0], place[1]
    half = out.shape[2]
    total = None
    for a in range(3):
        index = color ^ a
        first, second = mine[index], other[index]
        for h in range(2):
            weights = jnp.where(core == h, first, second)
            part = jnp.dot(
                stacked[a][:, h * half : (h + 1) * half], weights, preferred_element_type=F32
            )
            total = part if total is None else total + part
    sums = [total[:, b * half : (b + 1) * half] for b in range(3)]
    finish_conv(sums, block.shape[2], out)


def convolve(body, low, block, high, weights, place=()):
    frames, rows, width, channels = block.shape
    step = 4
    half = channels // 2

    def edge(count):
        return pl.BlockSpec((step, count, width, channels), lambda i, *_: (i, 0, 0, 0))

    def whole(value):
        return pl.BlockSpec(value.shape, lambda i, *_: (0,) * value.ndim)

    return pl.pallas_call(
        body,
        grid_spec=pltpu.PrefetchScalarGridSpec(
            num_scalar_prefetch=len(place),
            grid=(frames // step,),
            in_specs=[edge(1), edge(rows), edge(1)] + [whole(value) for value in weights],
            out_specs=pl.BlockSpec((step, rows * width, half), lambda i, *_: (i, 0, 0)),
        ),
        out_shape=jax.ShapeDtypeStruct((frames, rows * width, half), BF),
        compiler_params=pltpu.CompilerParams(vmem_limit_bytes=32 * 1024 * 1024),
        cost_estimate=pl.CostEstimate(
            flops=2 * frames * rows * width * 9 * channels * half,
            bytes_accessed=2 * (block.size * 2 + 9 * channels * half + block.size // 2),
            transcendentals=0,
        ),
        name="conv",
    )(*place, low, block, high, *weights)


def pack_body(half_of, weights, bias, tiles, rows, columns, counts, packed, selector):
    neurons, channels = weights.shape
    slots = packed.shape[0]
    half = channels // 2
    ids = jnp.broadcast_to(tiles[...], (neurons, neurons))
    before = lax.broadcasted_iota(jnp.int32, ids.shape, 0) < lax.broadcasted_iota(
        jnp.int32, ids.shape, 1
    )
    same = ids == jnp.transpose(ids)
    rank = jnp.sum(jnp.where(same & before, 1, 0), axis=0, keepdims=True)
    spot = tiles[...] * CAPACITY + rank
    chosen = jnp.where(
        lax.broadcasted_iota(jnp.int32, (slots, neurons), 0) == spot, 1.0, 0.0
    ).astype(BF)
    selector[...] = chosen
    lower, upper = weights[:, :half], weights[:, half:]
    own = jnp.where(half_of[0] == 0, lower, upper)
    far = jnp.where(half_of[0] == 0, upper, lower)
    packed[:, :half] = jnp.dot(chosen, own, preferred_element_type=F32).astype(BF)
    packed[:, half:channels] = jnp.dot(chosen, far, preferred_element_type=F32).astype(BF)
    lines = jnp.concatenate(
        [
            bias[...].astype(F32),
            (rows[...] * WIDTH + columns[...]).astype(F32),
            jnp.ones((1, neurons), F32),
            jnp.zeros((5, neurons), F32),
            counts[...].astype(F32),
            jnp.zeros((packed.shape[1] - channels - 8 - counts.shape[0], neurons), F32),
        ]
    ).astype(BF)
    packed[:, channels:] = lax.dot_general(
        chosen, lines, (((1,), (1,)), ((), ())), preferred_element_type=F32
    ).astype(BF)


def pack(half_of, weights, bias, tiles, rows, columns, counts, slots):
    neurons = weights.shape[0]
    smem = pl.BlockSpec(memory_space=pltpu.SMEM)
    vmem = pl.BlockSpec(memory_space=pltpu.VMEM)
    return pl.pallas_call(
        pack_body,
        in_specs=[smem] + [vmem] * 6,
        out_specs=[vmem, vmem],
        out_shape=[
            jax.ShapeDtypeStruct((slots, PACK), BF),
            jax.ShapeDtypeStruct((slots, neurons), BF),
        ],
        name="pack",
    )(half_of, weights, bias, tiles, rows, columns, counts)


def compute(
    acts,
    spatial_weight,
    temporal_weight,
    readout_weight,
    readout_bias,
    tile_of,
    row_of,
    column_of,
    spikes,
):
    fsdp = lax.axis_index("fsdp")
    block, mine_blocks, other_blocks, place = blocks_of(spatial_weight, temporal_weight)
    frames_in = acts[0, 0]
    frames, rows, width, channels = frames_in.shape
    half = channels // 2
    cells = rows * width
    tile_count = lax.axis_size("z") * lax.axis_size("x") * lax.axis_size("core")
    rep_count = lax.axis_size("fsdp")
    neurons = readout_weight.shape[1]
    capacity = CAPACITY
    slot_count = tile_count * capacity
    scale_factor = 1.0 / (rep_count * frames)
    low, high = edges(frames_in)

    def local(value):
        return jnp.where(
            fsdp == 0, value, jnp.concatenate([value[:, half:], value[:, :half]], axis=1)
        )

    packed, selector = pack(
        fsdp.astype(jnp.int32).reshape(1),
        readout_weight[0],
        readout_bias,
        tile_of.reshape(1, neurons),
        row_of,
        column_of,
        spikes[0, 0],
        slot_count,
    )
    held = lax.all_to_all(
        packed.reshape(tile_count, capacity, PACK),
        TILE,
        split_axis=0,
        concat_axis=0,
        tiled=True,
    ).reshape(slot_count, PACK)
    shifted_rows = [
        jnp.concatenate([low, frames_in[:, :1]], axis=1).reshape(-1, channels),
        frames_in.reshape(-1, channels),
        jnp.concatenate([frames_in[:, 1:], high], axis=1).reshape(-1, channels),
    ]
    near_out = convolve(near_body, low, frames_in, high, (spatial_weight,))
    far_out = convolve(
        far_body, low, frames_in, high, (mine_blocks, other_blocks), (place,)
    )
    far_out, held = lax.optimization_barrier((far_out, held))
    spatial_out = jnp.concatenate([near_out, far_out], axis=2)
    slot_weight = held[:, :channels]
    extras = held[:, channels : channels + 8 + frames].astype(F32)
    slot_bias = extras[:, :1]
    slot_cell = jnp.where(extras[:, 2:3] > 0.5, extras[:, 1:2].astype(jnp.int32), cells)
    slot_spikes = extras[:, 8:]

    lag_blocks = [block(q ^ fsdp, 3) for q in range(2)]
    temporal = [
        jnp.concatenate(
            [
                jnp.concatenate(
                    [
                        lax.dynamic_slice_in_dim(temporal_weight[lag], (q ^ fsdp) * half, half, 0),
                        lag_blocks[q][:, lag * half : (lag + 1) * half],
                    ],
                    axis=1,
                )
                for q in range(2)
            ]
        )
        for lag in range(3)
    ]
    causal = jnp.pad(spatial_out, ((2, 0), (0, 0), (0, 0)))
    mixed = jnp.zeros((frames * cells, channels), F32)
    for lag in range(3):
        mixed = mixed + jnp.dot(
            causal[2 - lag : 2 - lag + frames].reshape(-1, channels),
            temporal[lag],
            preferred_element_type=F32,
        )
    features = jax.nn.elu(mixed).astype(BF)

    here = slot_cell == jnp.arange(cells)[None, :]
    scores = lax.dot_general(
        slot_weight, features, (((1,), (1,)), ((), ())), preferred_element_type=F32
    ).reshape(slot_count, frames, cells)
    logits = jnp.sum(jnp.where(here[:, None, :], scores, 0.0), axis=2) + slot_bias
    delta = (jnp.exp(logits) - slot_spikes) * scale_factor
    coarse = lax.reduce_precision(delta, 8, 7)
    spread, rest = (
        jnp.where(here[:, None, :], piece.astype(BF)[:, :, None], jnp.zeros((), BF)).reshape(
            slot_count, -1
        )
        for piece in (coarse, delta - coarse)
    )
    feature_grad = contract_rows(
        jnp.concatenate([spread, rest]), jnp.concatenate([slot_weight, slot_weight])
    )
    slope = jnp.where(mixed > 0, 1.0, jnp.exp(jnp.minimum(mixed, 0.0)))
    mixed_grad = (feature_grad * slope).astype(BF)
    back_pad = jnp.pad(mixed_grad.reshape(frames, cells, channels), ((0, 2), (0, 0), (0, 0)))
    later = jnp.concatenate(
        [back_pad[lag : lag + frames].reshape(-1, channels) for lag in range(3)], axis=1
    )
    grad_t = contract_rows(spatial_out.reshape(-1, channels), later)
    slot_grad = jnp.dot(spread, features, preferred_element_type=F32)
    slot_bias_grad = jnp.sum(delta, axis=1, keepdims=True)
    back = jnp.concatenate(
        [slot_grad, slot_bias_grad, jnp.zeros((slot_count, PACK - channels - 1), F32)],
        axis=1,
    ).astype(BF)
    back = lax.optimization_barrier(back)

    spatial_back = lax.dot_general(
        later,
        jnp.concatenate(temporal, axis=1),
        (((1,), (1,)), ((), ())),
        preferred_element_type=F32,
    )
    spatial_back = spatial_back.reshape(frames, rows, width, channels)
    wider = jnp.concatenate(
        [shift(spatial_back, 1 - b).astype(BF).reshape(-1, channels) for b in range(3)], axis=1
    )
    grad_0 = contract_rows(shifted_rows[0], wider)
    first_part = reduce_first((grad_t, grad_0), (fsdp, 0))
    grad_1 = contract_rows(shifted_rows[1], wider)
    first_part, wider = lax.optimization_barrier((first_part, wider))
    grad_2 = contract_rows(shifted_rows[2], wider)
    second_part = reduce_first((grad_1, grad_2), (0, 0))
    middle = reduce_middle(jnp.concatenate([reduce_rows(first_part), reduce_rows(second_part)]))

    returned = lax.all_to_all(
        back.reshape(tile_count, capacity, PACK), TILE, split_axis=0, concat_axis=0, tiled=True
    ).reshape(slot_count, PACK)
    returned, middle = lax.optimization_barrier((returned, middle))
    mine = contract_rows(selector, returned)
    mine = jnp.concatenate([local(mine[:, :channels]), mine[:, channels:]], axis=1).astype(BF)
    other = lax.ppermute(mine, "fsdp", [(0, 1), (1, 0)])
    total = reduce_last(middle)
    summed = mine.astype(F32) + other.astype(F32)
    weight_grad = summed[:, :channels]
    bias_grad = summed[:, channels]

    def taps(value):
        return [value[:, b * half : (b + 1) * half].astype(F32) for b in range(3)]

    total_temporal = jnp.stack(taps(total[0]))
    total_spatial = jnp.stack(taps(total[1]) + taps(total[2]) + taps(total[3]))
    return (total_spatial, total_temporal, weight_grad[None], bias_grad[None])


def solution(mesh):
    shape = mesh.devices.shape
    split = Mesh(
        mesh.devices.reshape(shape[0], 4, 4, 2, shape[2]), ("fsdp", "z", "x", "core", "scan")
    )
    return jax.shard_map(
        compute,
        mesh=split,
        in_specs=(
            P("scan", "fsdp", None, TILE, None, None),
            P(None, None, "fsdp"),
            P(None, None, "fsdp"),
            P("scan", TILE, None),
            P("scan", TILE),
            P("scan", TILE, None),
            P("scan", TILE),
            P("scan", TILE),
            P("scan", "fsdp", None, TILE),
        ),
        out_specs=(
            P(None, None, "fsdp"),
            P(None, None, "fsdp"),
            P("scan", TILE, None),
            P("scan", TILE),
        ),
        check_vma=False,
    )
```

```python
import math

import jax
import jax.numpy as jnp
from jax import lax
from jax.experimental import pallas as pl
from jax.experimental.pallas import tpu as pltpu
from jax.sharding import Mesh, PartitionSpec as P


BF = jnp.bfloat16
F32 = jnp.float32
TILE = ("z", "x", "core")
ALL = ("fsdp", "z", "x", "core", "scan")
PACK = 640
CAPACITY = 10
WIDTH = 64


def contract_rows(left, right):
    return lax.dot_general(left, right, (((0,), (0,)), ((), ())), preferred_element_type=F32)


def swap(value, axis, kind):
    if axis == "core":
        pairs = ((0, 1),)
    elif kind == 0:
        pairs = ((0, 1), (2, 3))
    else:
        pairs = ((1, 2), (3, 0))
    name = ("fsdp", "scan") if axis == "y" else axis
    perm = [pair for a, b in pairs for pair in ((a, b), (b, a))]
    return lax.ppermute(value, name, perm)


def bit(axis, kind):
    if axis == "core":
        return lax.axis_index("core")
    if axis == "y":
        place = lax.axis_index("fsdp") * 2 + lax.axis_index("scan")
    else:
        place = lax.axis_index(axis)
    return place >> 1 if kind else (place ^ (place >> 1)) & 1


def permute_by_core(value, axes, flip):
    sizes = [lax.axis_size(name) for name in ALL]
    perm = []
    for index in range(math.prod(sizes)):
        rest, spot = index, {}
        for name, size in zip(reversed(ALL), reversed(sizes)):
            spot[name] = rest % size
            rest //= size
        spot["y"] = spot["fsdp"] * 2 + spot["scan"]
        spot[axes[spot["core"]]] ^= flip
        spot["fsdp"], spot["scan"] = spot["y"] // 2, spot["y"] % 2
        target = 0
        for name, size in zip(ALL, sizes):
            target = target * size + spot[name]
        perm.append((index, target))
    return lax.ppermute(value, ALL, perm)


def place_by_core(axes):
    first, second = (lax.axis_index(axis) for axis in axes)
    return jnp.where(lax.axis_index("core") == 0, first, second)


def quarter(value, axes):
    size = value.shape[1] // 4
    mine = place_by_core(axes)
    total = lax.dynamic_slice_in_dim(value, mine * size, size, 1)
    for flip in (1, 3, 2):
        sent = lax.dynamic_slice_in_dim(value, (mine ^ flip) * size, size, 1)
        total = total + permute_by_core(sent.astype(BF), axes, flip).astype(F32)
    return total


def sum_columns(value):
    cols = value.shape[2] // 6
    own, far = (
        jnp.concatenate([value[:, :, (2 * g + h) * cols :][:, :, :cols] for g in range(3)], axis=2)
        for h in range(2)
    )
    own, far = own.astype(BF), far.astype(BF)
    near = permute_by_core(own, ("y", "y"), 1)
    across = permute_by_core(far, ("y", "y"), 3)
    opposite = permute_by_core(far, ("y", "y"), 2)
    return (own.astype(F32) + near.astype(F32)) + (across.astype(F32) + opposite.astype(F32))


def regather(value, axes):
    mine = place_by_core(axes)
    got = [value] + [permute_by_core(value, axes, flip) for flip in (1, 2, 3)]
    pieces = []
    for spot in range(4):
        flip = mine ^ spot
        pieces.append(
            jnp.where(
                flip < 2,
                jnp.where(flip == 0, got[0], got[1]),
                jnp.where(flip == 2, got[2], got[3]),
            )
        )
    return jnp.concatenate(pieces, axis=1)


def joined(value, other, mine):
    first = mine == 0
    return jnp.concatenate(
        [jnp.where(first, value, other), jnp.where(first, other, value)], axis=1
    )


def reduce_first(grads, flips):
    core = lax.axis_index("core")
    size = grads[0].shape[0] // 2
    kept, sent = (
        jnp.stack(
            [
                lax.dynamic_slice_in_dim(grad, (core ^ flip ^ far) * size, size, 0)
                for grad, flip in zip(grads, flips)
            ]
        )
        for far in range(2)
    )
    return kept + swap(sent.astype(BF), "core", 0).astype(F32)


def reduce_rows(value):
    return quarter(value, ("x", "z"))


def reduce_middle(value):
    value = quarter(value, ("z", "x"))
    return sum_columns(value).astype(BF)


def reduce_last(value):
    value = regather(value, ("z", "x"))
    value = regather(value, ("x", "z"))
    return joined(value, swap(value, "core", 0), lax.axis_index("core"))


def blocks_of(spatial, temporal):
    color = bit("z", 0) ^ (bit("z", 1) * 2) ^ (bit("y", 0) * 3)
    rows, cols = spatial.shape[1] // 2, spatial.shape[2]
    core = lax.axis_index("core")
    start = core * rows
    taps = lax.dynamic_slice(spatial, (3 * jnp.minimum(color, 2), start, 0), (3, rows, cols))
    lags = lax.dynamic_slice_in_dim(temporal, start, rows, 1)
    part = jnp.where(color == 3, lags, taps)
    part = jnp.concatenate([part[0], part[1], part[2]], axis=1)
    part = swap(part, "y", 1)
    parts = [part, swap(part, "z", 0), swap(part, "z", 1), swap(part, "y", 0)]
    mine = jnp.stack(parts)
    other = swap(mine, "core", 0)

    def block(half, group):
        first, second = (
            lax.dynamic_index_in_dim(value, group ^ color, 0, False) for value in (mine, other)
        )
        return jnp.where(half == core, first, second)

    return block, mine, other, jnp.stack([core, color]).astype(jnp.int32)


def edges(block):
    count = 1
    for axis in TILE:
        count *= lax.axis_size(axis)
    forward = [(i, i + 1) for i in range(count - 1)]
    backward = [(b, a) for a, b in forward]
    low = lax.ppermute(block[:, -1:], TILE, forward)
    high = lax.ppermute(block[:, :1], TILE, backward)
    return low, high


def shift(value, step):
    if step == 0:
        return value
    zeros = jnp.zeros_like(value[:, :, :1])
    if step > 0:
        return jnp.concatenate([value[:, :, 1:], zeros], axis=2)
    return jnp.concatenate([zeros, value[:, :, :-1]], axis=2)


def stacked_rows(low, block, high):
    count, rows, width, channels = block.shape
    parts = (
        jnp.concatenate([low[...], block[:, :1]], axis=1),
        block[...],
        jnp.concatenate([block[:, 1:], high[...]], axis=1),
    )
    return [part.reshape(count * rows * width, channels) for part in parts]


def finish_conv(sums, width, out):
    left, middle, right = sums
    size = left.shape[0]
    column = lax.broadcasted_iota(jnp.int32, left.shape, 0) % width
    left = jnp.where(column == 0, 0.0, pltpu.roll(left, 1, 0))
    right = jnp.where(column == width - 1, 0.0, pltpu.roll(right, size - 1, 0))
    out[...] = (left + middle + right).astype(BF).reshape(out.shape)


def near_body(low, block, high, weights, out):
    stacked = stacked_rows(low, block, high)
    sums = []
    for b in range(3):
        total = None
        for a in range(3):
            part = jnp.dot(stacked[a], weights[3 * a + b], preferred_element_type=F32)
            total = part if total is None else total + part
        sums.append(total)
    finish_conv(sums, block.shape[2], out)


def far_body(place, low, block, high, mine, other, out):
    stacked = stacked_rows(low, block, high)
    core, color = place[0], place[1]
    half = out.shape[2]
    total = None
    for a in range(3):
        index = color ^ a
        first, second = mine[index], other[index]
        for h in range(2):
            weights = jnp.where(core == h, first, second)
            part = jnp.dot(
                stacked[a][:, h * half : (h + 1) * half], weights, preferred_element_type=F32
            )
            total = part if total is None else total + part
    sums = [total[:, b * half : (b + 1) * half] for b in range(3)]
    finish_conv(sums, block.shape[2], out)


def convolve(body, low, block, high, weights, place=()):
    frames, rows, width, channels = block.shape
    step = 4
    half = channels // 2

    def edge(count):
        return pl.BlockSpec((step, count, width, channels), lambda i, *_: (i, 0, 0, 0))

    def whole(value):
        return pl.BlockSpec(value.shape, lambda i, *_: (0,) * value.ndim)

    return pl.pallas_call(
        body,
        grid_spec=pltpu.PrefetchScalarGridSpec(
            num_scalar_prefetch=len(place),
            grid=(frames // step,),
            in_specs=[edge(1), edge(rows), edge(1)] + [whole(value) for value in weights],
            out_specs=pl.BlockSpec((step, rows * width, half), lambda i, *_: (i, 0, 0)),
        ),
        out_shape=jax.ShapeDtypeStruct((frames, rows * width, half), BF),
        compiler_params=pltpu.CompilerParams(vmem_limit_bytes=32 * 1024 * 1024),
        cost_estimate=pl.CostEstimate(
            flops=2 * frames * rows * width * 9 * channels * half,
            bytes_accessed=2 * (block.size * 2 + 9 * channels * half + block.size // 2),
            transcendentals=0,
        ),
        name="conv",
    )(*place, low, block, high, *weights)


def pack_body(half_of, weights, bias, tiles, rows, columns, counts, packed, selector):
    neurons, channels = weights.shape
    slots = packed.shape[0]
    half = channels // 2
    ids = jnp.broadcast_to(tiles[...], (neurons, neurons))
    before = lax.broadcasted_iota(jnp.int32, ids.shape, 0) < lax.broadcasted_iota(
        jnp.int32, ids.shape, 1
    )
    same = ids == jnp.transpose(ids)
    rank = jnp.sum(jnp.where(same & before, 1, 0), axis=0, keepdims=True)
    spot = tiles[...] * CAPACITY + rank
    chosen = jnp.where(
        lax.broadcasted_iota(jnp.int32, (slots, neurons), 0) == spot, 1.0, 0.0
    ).astype(BF)
    selector[...] = chosen
    lower, upper = weights[:, :half], weights[:, half:]
    own = jnp.where(half_of[0] == 0, lower, upper)
    far = jnp.where(half_of[0] == 0, upper, lower)
    packed[:, :half] = jnp.dot(chosen, own, preferred_element_type=F32).astype(BF)
    packed[:, half:channels] = jnp.dot(chosen, far, preferred_element_type=F32).astype(BF)
    lines = jnp.concatenate(
        [
            bias[...].astype(F32),
            (rows[...] * WIDTH + columns[...]).astype(F32),
            jnp.ones((1, neurons), F32),
            jnp.zeros((5, neurons), F32),
            counts[...].astype(F32),
            jnp.zeros((packed.shape[1] - channels - 8 - counts.shape[0], neurons), F32),
        ]
    ).astype(BF)
    packed[:, channels:] = lax.dot_general(
        chosen, lines, (((1,), (1,)), ((), ())), preferred_element_type=F32
    ).astype(BF)


def pack(half_of, weights, bias, tiles, rows, columns, counts, slots):
    neurons = weights.shape[0]
    smem = pl.BlockSpec(memory_space=pltpu.SMEM)
    vmem = pl.BlockSpec(memory_space=pltpu.VMEM)
    return pl.pallas_call(
        pack_body,
        in_specs=[smem] + [vmem] * 6,
        out_specs=[vmem, vmem],
        out_shape=[
            jax.ShapeDtypeStruct((slots, PACK), BF),
            jax.ShapeDtypeStruct((slots, neurons), BF),
        ],
        name="pack",
    )(half_of, weights, bias, tiles, rows, columns, counts)


def compute(
    acts,
    spatial_weight,
    temporal_weight,
    readout_weight,
    readout_bias,
    tile_of,
    row_of,
    column_of,
    spikes,
):
    fsdp = lax.axis_index("fsdp")
    block, mine_blocks, other_blocks, place = blocks_of(spatial_weight, temporal_weight)
    frames_in = acts[0, 0]
    frames, rows, width, channels = frames_in.shape
    half = channels // 2
    cells = rows * width
    tile_count = lax.axis_size("z") * lax.axis_size("x") * lax.axis_size("core")
    rep_count = lax.axis_size("fsdp")
    neurons = readout_weight.shape[1]
    capacity = CAPACITY
    slot_count = tile_count * capacity
    scale_factor = 1.0 / (rep_count * frames)
    low, high = edges(frames_in)

    def local(value):
        return jnp.where(
            fsdp == 0, value, jnp.concatenate([value[:, half:], value[:, :half]], axis=1)
        )

    packed, selector = pack(
        fsdp.astype(jnp.int32).reshape(1),
        readout_weight[0],
        readout_bias,
        tile_of.reshape(1, neurons),
        row_of,
        column_of,
        spikes[0, 0],
        slot_count,
    )
    held = lax.all_to_all(
        packed.reshape(tile_count, capacity, PACK),
        TILE,
        split_axis=0,
        concat_axis=0,
        tiled=True,
    ).reshape(slot_count, PACK)
    shifted_rows = [
        jnp.concatenate([low, frames_in[:, :1]], axis=1).reshape(-1, channels),
        frames_in.reshape(-1, channels),
        jnp.concatenate([frames_in[:, 1:], high], axis=1).reshape(-1, channels),
    ]

    near_out = convolve(near_body, low, frames_in, high, (spatial_weight,))
    far_out = convolve(
        far_body, low, frames_in, high, (mine_blocks, other_blocks), (place,)
    )
    far_out, slot_weight, extras = lax.optimization_barrier(
        (far_out, held[:, :channels], held[:, channels:])
    )
    spatial_out = jnp.concatenate([near_out, far_out], axis=2)
    extras = extras[:, : 8 + frames].astype(F32)
    slot_bias = extras[:, :1]
    slot_cell = jnp.where(extras[:, 2:3] > 0.5, extras[:, 1:2].astype(jnp.int32), cells)
    slot_spikes = extras[:, 8:]

    lag_blocks = [block(q ^ fsdp, 3) for q in range(2)]
    temporal = [
        jnp.concatenate(
            [
                jnp.concatenate(
                    [
                        lax.dynamic_slice_in_dim(temporal_weight[lag], (q ^ fsdp) * half, half, 0),
                        lag_blocks[q][:, lag * half : (lag + 1) * half],
                    ],
                    axis=1,
                )
                for q in range(2)
            ]
        )
        for lag in range(3)
    ]
    causal = jnp.pad(spatial_out, ((2, 0), (0, 0), (0, 0)))
    mixed = jnp.zeros((frames * cells, channels), F32)
    for lag in range(3):
        mixed = mixed + jnp.dot(
            causal[2 - lag : 2 - lag + frames].reshape(-1, channels),
            temporal[lag],
            preferred_element_type=F32,
        )
    features = jax.nn.elu(mixed).astype(BF)

    here = slot_cell == jnp.arange(cells)[None, :]
    scores = lax.dot_general(
        slot_weight, features, (((1,), (1,)), ((), ())), preferred_element_type=F32
    ).reshape(slot_count, frames, cells)
    logits = jnp.sum(jnp.where(here[:, None, :], scores, 0.0), axis=2) + slot_bias
    delta = (jnp.exp(logits) - slot_spikes) * scale_factor
    coarse = lax.reduce_precision(delta, 8, 7)
    spread, rest = (
        jnp.where(here[:, None, :], piece.astype(BF)[:, :, None], jnp.zeros((), BF)).reshape(
            slot_count, -1
        )
        for piece in (coarse, delta - coarse)
    )
    feature_grad = contract_rows(
        jnp.concatenate([spread, rest]), jnp.concatenate([slot_weight, slot_weight])
    )
    slope = jnp.where(mixed > 0, 1.0, jnp.exp(jnp.minimum(mixed, 0.0)))
    mixed_grad = (feature_grad * slope).astype(BF)
    back_pad = jnp.pad(mixed_grad.reshape(frames, cells, channels), ((0, 2), (0, 0), (0, 0)))
    later = jnp.concatenate(
        [back_pad[lag : lag + frames].reshape(-1, channels) for lag in range(3)], axis=1
    )
    grad_t = contract_rows(spatial_out.reshape(-1, channels), later)
    slot_grad = jnp.dot(spread, features, preferred_element_type=F32)
    slot_bias_grad = jnp.sum(delta, axis=1, keepdims=True)
    back = jnp.concatenate(
        [slot_grad, slot_bias_grad, jnp.zeros((slot_count, PACK - channels - 1), F32)],
        axis=1,
    ).astype(BF)
    back = lax.optimization_barrier(back)

    spatial_back = lax.dot_general(
        later,
        jnp.concatenate(temporal, axis=1),
        (((1,), (1,)), ((), ())),
        preferred_element_type=F32,
    )
    spatial_back = spatial_back.reshape(frames, rows, width, channels)
    wider = jnp.concatenate(
        [shift(spatial_back, 1 - b).astype(BF).reshape(-1, channels) for b in range(3)], axis=1
    )
    grad_0 = contract_rows(shifted_rows[0], wider)
    first_part = reduce_first((grad_t, grad_0), (fsdp, 0))
    grad_1 = contract_rows(shifted_rows[1], wider)
    first_part, wider = lax.optimization_barrier((first_part, wider))
    grad_2 = contract_rows(shifted_rows[2], wider)
    second_part = reduce_first((grad_1, grad_2), (0, 0))
    middle = reduce_middle(jnp.concatenate([reduce_rows(first_part), reduce_rows(second_part)]))

    returned = lax.all_to_all(
        back.reshape(tile_count, capacity, PACK), TILE, split_axis=0, concat_axis=0, tiled=True
    ).reshape(slot_count, PACK)
    returned, middle = lax.optimization_barrier((returned, middle))
    mine = contract_rows(selector, returned)
    mine = jnp.concatenate([local(mine[:, :channels]), mine[:, channels:]], axis=1).astype(BF)
    other = lax.ppermute(mine, "fsdp", [(0, 1), (1, 0)])
    total = reduce_last(middle)
    summed = mine.astype(F32) + other.astype(F32)
    weight_grad = summed[:, :channels]
    bias_grad = summed[:, channels]

    def taps(value):
        return [value[:, b * half : (b + 1) * half].astype(F32) for b in range(3)]

    total_temporal = jnp.stack(taps(total[0]))
    total_spatial = jnp.stack(taps(total[1]) + taps(total[2]) + taps(total[3]))
    return (total_spatial, total_temporal, weight_grad[None], bias_grad[None])


def solution(mesh):
    shape = mesh.devices.shape
    split = Mesh(
        mesh.devices.reshape(shape[0], 4, 4, 2, shape[2]), ("fsdp", "z", "x", "core", "scan")
    )
    return jax.shard_map(
        compute,
        mesh=split,
        in_specs=(
            P("scan", "fsdp", None, TILE, None, None),
            P(None, None, "fsdp"),
            P(None, None, "fsdp"),
            P("scan", TILE, None),
            P("scan", TILE),
            P("scan", TILE, None),
            P("scan", TILE),
            P("scan", TILE),
            P("scan", "fsdp", None, TILE),
        ),
        out_specs=(
            P(None, None, "fsdp"),
            P(None, None, "fsdp"),
            P("scan", TILE, None),
            P("scan", TILE),
        ),
        check_vma=False,
    )
```
